256 devices in a mesh: grp: 8 (over y, z_hi), tp: 4 (over z_lo), ffn: 8 (over x, core).
Axes of the slice: x: 4, y: 4, z: 8 (z_hi: 2, z_lo: 4; z = z_hi * 4 + z_lo), core: 2. Of those that a mesh axis runs over, the one named last changes fastest.
Arguments:
- queries: bfloat16 [768, 8192], P('grp', 'tp'), may hold values from -320 to 320
- new_kv: bfloat16 [2, 768, 1024], P(None, 'grp', 'tp'), may hold values from -12 to 12
- kv_cache: bfloat16 [2, 8, 16384, 1024], P(None, 'grp', 'ffn', 'tp'), may hold values from -12 to 12
- lengths: int32 [8], P('grp'), may hold values from 1 to 96, as said below
- prefixes: int32 [8], P('grp'), may hold values from 0 to 16384, as said below
- resid: bfloat16 [768, 8192], P('grp', 'ffn'), may hold values from -0.29882812 to 0.29882812
- out_weight: bfloat16 [8192, 8192], P('tp', 'ffn'), may hold values from -0.0625 to 0.0625
- gain: bfloat16 [8192], P('ffn'), may hold values from 0.099609375 to 1.8984375
- gate_weight: bfloat16 [8192, 29568], P('ffn', ('grp', 'tp')), may hold values from -0.0625 to 0.0625
- up_weight: bfloat16 [8192, 29568], P('ffn', ('grp', 'tp')), may hold values from -0.0625 to 0.0625
- down_weight: bfloat16 [29568, 8192], P(('grp', 'tp'), 'ffn'), may hold values from -0.03125 to 0.03125
Outputs:
- layer_out: bfloat16 [768, 8192], P(('grp', 'tp'), 'ffn')
The draws below stay inside these ranges and needn't reach their ends.
Inputs may be any that keep to these rules, and one draw needn't show every extreme that they name: `lengths`: some group has a full block of 96 live slots. `prefixes`: some group has all 16384 cached positions in use.
All inputs are finite; a program needn't handle non-finite values.
Results may differ from the reference program's by a relative error of at most 0.02.
Values may be sent and summed in bfloat16 or wider, within the bound.
A program may use at most 64 MiB of HBM per device.

```python
import jax
import jax.numpy as jnp
from jax import lax

D = 8192
HQ = 64
KVH = 8
DH = 128
FF = 29568
SPAN = 96
TOKENS = 768
CACHE = 16384
N_GRP = 8


def on_grid(values):
    return jnp.floor(values * 16.0) / 16.0


def draw_queries(key, part):
    values = on_grid(jnp.clip(jax.random.normal(key, (TOKENS, HQ * DH), jnp.float32), -5.0, 5.0))
    return values.astype(jnp.bfloat16)


def draw_new_kv(key, part):
    values = 2.0 * jax.random.normal(jax.random.fold_in(key, 31), (2, TOKENS, KVH * DH), jnp.float32)
    return on_grid(jnp.clip(values, -11.9, 11.9)).astype(jnp.bfloat16)


def draw_kv_cache(key, part):
    values = 2.0 * jax.random.normal(jax.random.fold_in(key, 37), (2, N_GRP, CACHE, KVH * DH), jnp.float32)
    return on_grid(jnp.clip(values, -11.9, 11.9)).astype(jnp.bfloat16)


def draw_lengths(key, part):
    first, second = jax.random.split(jax.random.fold_in(key, 11))
    values = jax.random.randint(first, (N_GRP,), 1, SPAN + 1, dtype=jnp.int32)
    spot = jax.random.randint(second, (), 0, N_GRP, dtype=jnp.int32)
    return values.at[spot].set(SPAN)


def draw_prefixes(key, part):
    first, second = jax.random.split(jax.random.fold_in(key, 23))
    values = jax.random.randint(first, (N_GRP,), 0, CACHE + 1, dtype=jnp.int32)
    spot = jax.random.randint(second, (), 0, N_GRP, dtype=jnp.int32)
    return values.at[spot].set(CACHE)


def steps_of(stream_key, shape, pieces, smallest, high):
    def one(dim, blocks):
        steps = jax.random.uniform(jax.random.fold_in(jax.random.fold_in(stream_key, 6), dim), (blocks,), jnp.float32, smallest / len(pieces), high / len(pieces))
        return jnp.repeat(jnp.exp(steps), shape[dim] // blocks).reshape((-1,) + (1,) * (len(shape) - dim - 1))

    factor_of = one(*pieces[0])
    for cut in pieces[1:]:
        factor_of = factor_of * one(*cut)
    return factor_of


def gaussian(key, shape, scale, bound, cuts=(), held_as=jnp.bfloat16):
    entries = jax.random.normal(key, shape, jnp.float32) * scale
    if len(cuts) > 0:
        entries = steps_of(key, shape, cuts, -0.22, 0.18) * entries
    return jnp.clip(entries, min=-bound, max=bound).astype(held_as)


def setup_inputs(seed: int = 0) -> dict:
    seeds = jax.random.split(jax.random.key(seed), 12)
    queries = draw_queries(jax.random.fold_in(seeds[11], 71), 0)
    new_kv = draw_new_kv(jax.random.fold_in(seeds[11], 71), 0)
    kv_cache = draw_kv_cache(jax.random.fold_in(seeds[11], 71), 0)
    lengths = draw_lengths(jax.random.fold_in(seeds[11], 71), 0)
    prefixes = draw_prefixes(jax.random.fold_in(seeds[11], 71), 0)
    resid = gaussian(seeds[5], (TOKENS, D), 0.05, 0.29882812, ((0, 8), (1, 8)))
    out_weight = gaussian(seeds[6], (HQ * DH, D), (HQ * DH) ** -0.5, 0.0625, ((0, 4), (1, 8)))
    gain = jnp.clip(1.0 + 0.18 * jax.random.normal(seeds[7], (D,), jnp.float32), 0.099609375, 1.8984375).astype(jnp.bfloat16)
    gate_weight = gaussian(seeds[8], (D, FF), D ** -0.5, 0.0625, ((0, 8), (1, 32)))
    up_weight = gaussian(seeds[9], (D, FF), D ** -0.5, 0.0625, ((0, 8), (1, 32)))
    down_weight = gaussian(seeds[10], (FF, D), FF ** -0.5, 0.03125, ((0, 32), (1, 8)))
    return {"queries": queries, "new_kv": new_kv, "kv_cache": kv_cache, "lengths": lengths, "prefixes": prefixes, "resid": resid, "out_weight": out_weight, "gain": gain, "gate_weight": gate_weight, "up_weight": up_weight, "down_weight": down_weight}


def attend_group(items):
    q_grp, kn_grp, vn_grp, kc_grp, vc_grp, length, prefix = items
    key_pos = jnp.arange(CACHE + SPAN, dtype=jnp.int32)[None, :]
    row_pos = jnp.arange(SPAN, dtype=jnp.int32)[:, None]
    new_pos = key_pos - CACHE
    valid = jnp.where(key_pos < CACHE, key_pos < prefix, (new_pos < length) & (new_pos <= row_pos))

    def attend_head(parts):
        q_head, kn_head, vn_head, kc_head, vc_head = parts
        keys = jnp.concatenate([kc_head.astype(jnp.float32), kn_head], axis=0)
        values = jnp.concatenate([vc_head.astype(jnp.float32), vn_head], axis=0)
        scores = jnp.einsum('gid,kd->gik', q_head, keys) / jnp.sqrt(jnp.float32(DH))
        scores = jnp.where(valid[None], scores, jnp.float32(-1e+30))
        top = lax.optimization_barrier(jnp.max(scores, axis=-1, keepdims=True))
        probs = jnp.where(valid[None], jnp.exp(scores - top), jnp.float32(0.0))
        total = lax.optimization_barrier(jnp.sum(probs, axis=-1, keepdims=True))
        return jnp.einsum('gik,kd->gid', probs, values) / total
    return lax.map(attend_head, (q_grp, kn_grp, vn_grp, kc_grp, vc_grp))

def reference(queries, new_kv, kv_cache, lengths, prefixes, resid, out_weight, gain, gate_weight, up_weight, down_weight):
    group = HQ // KVH
    q_all = queries.astype(jnp.float32).reshape(N_GRP, SPAN, KVH, group, DH).transpose(0, 2, 3, 1, 4)
    kn_all = new_kv[0].astype(jnp.float32).reshape(N_GRP, SPAN, KVH, DH).transpose(0, 2, 1, 3)
    vn_all = new_kv[1].astype(jnp.float32).reshape(N_GRP, SPAN, KVH, DH).transpose(0, 2, 1, 3)
    kc_all = kv_cache[0].reshape(N_GRP, CACHE, KVH, DH).transpose(0, 2, 1, 3)
    vc_all = kv_cache[1].reshape(N_GRP, CACHE, KVH, DH).transpose(0, 2, 1, 3)
    heads = lax.map(attend_group, (q_all, kn_all, vn_all, kc_all, vc_all, lengths, prefixes))
    attn = heads.transpose(0, 3, 1, 2, 4).reshape(TOKENS, HQ * DH).astype(jnp.bfloat16)
    h1 = (jnp.dot(attn, out_weight, preferred_element_type=jnp.float32) + resid.astype(jnp.float32)).astype(jnp.bfloat16)
    h1f = h1.astype(jnp.float32)
    squares = lax.optimization_barrier(jnp.sum(h1f * h1f, axis=1))
    inv_rms = lax.rsqrt(squares / D + 1e-06)
    scaled = (h1f * gain.astype(jnp.float32)[None, :]).astype(jnp.bfloat16)
    gate = jnp.dot(scaled, gate_weight, preferred_element_type=jnp.float32) * inv_rms[:, None]
    upper = jnp.dot(scaled, up_weight, preferred_element_type=jnp.float32) * inv_rms[:, None]
    hidden = (jax.nn.silu(gate) * upper).astype(jnp.bfloat16)
    down = jnp.dot(hidden, down_weight, preferred_element_type=jnp.float32)
    slot = jnp.arange(TOKENS, dtype=jnp.int32) % SPAN
    live = slot < jnp.repeat(lengths, SPAN)
    return jnp.where(live[:, None], h1f + down, jnp.float32(0.0)).astype(jnp.bfloat16)
```

```python
import functools
import math

import jax
import jax.numpy as jnp
from jax import lax
from jax.experimental import pallas as pl
from jax.experimental.pallas import tpu as pltpu
from jax.sharding import PartitionSpec as P

MESH = pl.DeviceIdType.MESH
F32 = jnp.float32
BF16 = jnp.bfloat16

D = 8192
DH = 128
SPAN = 96
ROWS_OUT = 24
KEYS = 2048
WIDTH = 1024
HID = 924
NEG = -1e30
SCALE = math.log2(math.e) / math.sqrt(DH)


class Place:
    def __init__(self):
        g = lax.axis_index("grp")
        self.t = lax.axis_index("tp")
        self.f = lax.axis_index("ffn")
        self.y, self.zh = g // 2, g % 2
        self.x, self.c = self.f // 2, self.f % 2
        self.z = self.zh * 4 + self.t
        self.xa, self.xb = flip(self.x), 3 - self.x
        self.ya, self.yb = flip(self.y), 3 - self.y

    def ffn(self, f):
        return {"ffn": f}

    def tp(self, t):
        return {"tp": t}

    def core(self):
        return {"ffn": self.x * 2 + 1 - self.c}

    def at_x(self, x):
        return {"ffn": x * 2 + self.c}

    def at_y(self, y):
        return {"grp": y * 2 + self.zh}

    def at_z(self, step):
        z = (self.z + step + 8) % 8
        return {"grp": self.y * 2 + z // 4, "tp": z % 4}


def flip(v):
    return v + 1 - 2 * (v % 2)


class Links:
    def __init__(self, send_sems, recv_sems):
        self.send_sems, self.recv_sems = send_sems, recv_sems
        self.started = []

    def start(self, src, dst, device):
        k = len(self.started)
        copy = pltpu.make_async_remote_copy(
            src_ref=src,
            dst_ref=dst,
            send_sem=self.send_sems.at[k],
            recv_sem=self.recv_sems.at[k],
            device_id=device,
            device_id_type=MESH,
        )
        copy.start()
        self.started.append(copy)
        return copy

    def finish(self):
        for copy in self.started:
            copy.wait_send()


def greet(devices):
    barrier = pltpu.get_barrier_semaphore()
    for device in devices:
        pl.semaphore_signal(barrier, inc=1, device_id=device, device_id_type=MESH)


def greeted(devices):
    pl.semaphore_wait(pltpu.get_barrier_semaphore(), len(devices))


def in_turn(*flows):
    alive = list(flows)
    while alive:
        for flow in list(alive):
            try:
                next(flow)
            except StopIteration:
                alive.remove(flow)


def arrived(*copies):
    for copy in copies:
        copy.wait_recv()


def attention_kernel(
    length_ref, prefix_ref, q_ref, new_ref, resid_ref, cache_hbm, wo_hbm,
    h_ref,
    kv, wo, o_out, st_out, o_in, st_in, att, part_f, part_b, part_in,
    local_sems, send_sems, recv_sems,
):
    me = Place()
    links = Links(send_sems, recv_sems)
    f, t, y, z = me.f, me.t, me.y, me.z
    load_k = pltpu.make_async_copy(cache_hbm.at[0, 0], kv.at[0], local_sems.at[0])
    load_v = pltpu.make_async_copy(cache_hbm.at[1, 0], kv.at[1], local_sems.at[1])
    load_wo = pltpu.make_async_copy(wo_hbm, wo, local_sems.at[2])
    load_k.start()
    load_v.start()
    load_wo.start()
    friends = [me.ffn((f + d) % 8) for d in range(1, 8)]
    friends += [me.tp((t + d) % 4) for d in range(1, 4)]
    friends += [me.at_y(me.ya), me.at_y(me.yb), me.at_z(1), me.at_z(-1)]
    greet(friends)

    length, prefix = length_ref[0], prefix_ref[0]
    lanes = lax.broadcasted_iota(jnp.int32, (1, KEYS), 1)
    bias = jnp.where(f * KEYS + lanes < prefix, 0.0, NEG).astype(F32)
    slot = lax.broadcasted_iota(jnp.int32, (SPAN, SPAN), 0)
    key = lax.broadcasted_iota(jnp.int32, (SPAN, SPAN), 1)
    limit = jnp.where(f == 0, length, 0)
    new_bias = jnp.where((key <= slot) & (key < limit), 0.0, NEG).astype(F32)
    new_bias = jnp.concatenate([new_bias] * 4, axis=0)
    lane = lax.broadcasted_iota(jnp.int32, (4 * SPAN, 128), 1)
    load_k.wait()
    load_v.wait()

    def attend(step, carry):
        half, h = step // 2, step % 2
        cols = pl.ds(pl.multiple_of(h * DH, DH), DH)
        keys, values = kv[0, :, cols], kv[1, :, cols]
        new_keys, new_values = new_ref[0, :, cols], new_ref[1, :, cols]
        q = jnp.concatenate(
            [
                q_ref[:, pl.ds(pl.multiple_of((h * 8 + half * 4 + i) * DH, DH), DH)]
                for i in range(4)
            ],
            axis=0,
        )
        nt = (((1,), (1,)), ((), ()))
        s = lax.dot_general(q, keys, nt, preferred_element_type=F32) + bias
        s_new = lax.dot_general(q, new_keys, nt, preferred_element_type=F32) + new_bias
        top = jnp.maximum(
            jnp.max(s, axis=1, keepdims=True), jnp.max(s_new, axis=1, keepdims=True)
        )
        p = jnp.exp2((s - top) * SCALE).astype(BF16)
        p_new = jnp.exp2((s_new - top) * SCALE).astype(BF16)
        wide = jnp.concatenate([values, jnp.ones((KEYS, DH), BF16)], axis=1)
        wide_new = jnp.concatenate([new_values, jnp.ones((SPAN, DH), BF16)], axis=1)
        acc = jnp.dot(p, wide, preferred_element_type=F32) + jnp.dot(
            p_new, wide_new, preferred_element_type=F32
        )
        total = acc[:, DH:]
        out = (acc[:, :DH] / total).astype(BF16)
        stats = jnp.where(lane == 0, top, jnp.where(lane == 1, total, 0.0))
        for i in range(4):
            rows = slice(i * SPAN, (i + 1) * SPAN)
            o_out[half * 4 + i, h] = out[rows]
            square = jnp.concatenate([stats[rows], jnp.zeros((32, 128), F32)], axis=0)
            st_out[half * 4 + i, h] = jnp.transpose(square)[:8]
        return carry

    lax.fori_loop(0, 4, attend, 0)

    greeted(friends)
    waits = []
    for d in range(1, 8):
        to = (f + d) % 8
        waits.append(links.start(st_out.at[to], st_in.at[d], me.ffn(to)))
        waits.append(links.start(o_out.at[to], o_in.at[d], me.ffn(to)))
    arrived(*waits)
    for h in range(2):
        stats = [st_out[f, h]] + [st_in[d, h] for d in range(1, 8)]
        tops = [s[0:1] for s in stats]
        top = functools.reduce(jnp.maximum, tops)
        weights = [s[1:2] * jnp.exp2((m - top) * SCALE) for s, m in zip(stats, tops)]
        total = sum(weights[1:], weights[0])
        shares = jnp.concatenate(
            [w / total for w in weights] + [jnp.zeros((120, 128), F32)], axis=0
        )
        shares = jnp.transpose(shares)[:SPAN]
        mine = o_out[f, h].astype(F32) * shares[:, 0:1]
        for d in range(1, 8):
            mine += o_in[d, h].astype(F32) * shares[:, d : d + 1]
        att[f, h] = mine.astype(BF16)
    arrived(*[links.start(att.at[f], att.at[f], me.ffn((f + d) % 8)) for d in range(1, 8)])

    load_wo.wait()
    attn = jnp.concatenate([att[q, h] for h in range(2) for q in range(8)], axis=1)
    part = jnp.dot(attn, wo[...], preferred_element_type=F32)
    for j in range(4):
        piece = part[:, j * 256 : (j + 1) * 256]
        part_f[j] = piece
        part_b[j] = piece.astype(BF16)
    waits = []
    for d in range(1, 4):
        to = (t + d) % 4
        waits.append(links.start(part_b.at[to], part_in.at[d - 1], me.tp(to)))
    arrived(*waits)
    h1 = part_f[t] + resid_ref[:, pl.ds(pl.multiple_of(t * 256, 256), 256)].astype(F32)
    for d in range(3):
        h1 += part_in[d].astype(F32)
    h1 = h1.astype(BF16)
    h_ref[0, z, y] = h1[:, :128]
    h_ref[1, z, y] = h1[:, 128:]

    def ring(part, whole, first, second):
        right = links.start(whole(part, z), whole(part, z), me.at_z(1))
        left = links.start(whole(part, z), whole(part, z), me.at_z(-1))
        yield
        for s in (1, 2):
            arrived(right)
            at = (z - s + 8) % 8
            right = links.start(whole(part, at), whole(part, at), me.at_z(1))
            arrived(left)
            at = (z + s) % 8
            left = links.start(whole(part, at), whole(part, at), me.at_z(-1))
            yield
        arrived(right)
        at = (z - 3 + 8) % 8
        right = links.start(first(part, at), first(part, at), me.at_z(1))
        arrived(left)
        at = (z + 3) % 8
        left = links.start(second(part, at), second(part, at), me.at_z(-1))
        yield
        arrived(right, left)

    pair = pl.ds(2 * (y // 2), 2)

    def y_first():
        one = links.start(h_ref.at[0, z, y], h_ref.at[0, z, y], me.at_y(me.ya))
        yield
        arrived(one)
        two = links.start(h_ref.at[0, z, pair], h_ref.at[0, z, pair], me.at_y(me.yb))
        yield
        arrived(two)
        yield from ring(
            0,
            lambda p, at: h_ref.at[p, at],
            lambda p, at: h_ref.at[p, at, pl.ds(0, 2)],
            lambda p, at: h_ref.at[p, at, pl.ds(2, 2)],
        )

    low, high = pl.ds(0, 48), pl.ds(48, 48)

    def z_first():
        yield from ring(
            1,
            lambda p, at: h_ref.at[p, at, y],
            lambda p, at: h_ref.at[p, at, y, low],
            lambda p, at: h_ref.at[p, at, y, high],
        )
        a = links.start(h_ref.at[1, :, y, low], h_ref.at[1, :, y, low], me.at_y(me.ya))
        b = links.start(h_ref.at[1, :, y, high], h_ref.at[1, :, y, high], me.at_y(me.yb))
        yield
        arrived(a)
        a = links.start(h_ref.at[1, :, pair, low], h_ref.at[1, :, pair, low], me.at_y(me.yb))
        arrived(b)
        b = links.start(h_ref.at[1, :, y, high], h_ref.at[1, :, y, high], me.at_y(me.ya))
        b2 = links.start(
            h_ref.at[1, :, me.yb, high], h_ref.at[1, :, me.yb, high], me.at_y(me.ya)
        )
        yield
        arrived(a, b, b2)

    in_turn(y_first(), z_first())
    links.finish()


def attention_call(lengths, prefixes, queries, new_kv, resid, kv_cache, out_weight):
    vmem = pl.BlockSpec(memory_space=pltpu.VMEM)
    smem = pl.BlockSpec(memory_space=pltpu.SMEM)
    hbm = pl.BlockSpec(memory_space=pl.ANY)
    copies = 7 * 3 + 3 + 2 + 8 + 8 + 5
    return pl.pallas_call(
        attention_kernel,
        out_shape=jax.ShapeDtypeStruct((2, 8, 4, SPAN, 128), BF16),
        in_specs=[smem, smem, vmem, vmem, vmem, hbm, hbm],
        out_specs=vmem,
        scratch_shapes=[
            pltpu.VMEM((2, KEYS, 256), BF16),
            pltpu.VMEM((2048, WIDTH), BF16),
            pltpu.VMEM((8, 2, SPAN, DH), BF16),
            pltpu.VMEM((8, 2, 8, 128), F32),
            pltpu.VMEM((8, 2, SPAN, DH), BF16),
            pltpu.VMEM((8, 2, 8, 128), F32),
            pltpu.VMEM((8, 2, SPAN, DH), BF16),
            pltpu.VMEM((4, SPAN, 256), F32),
            pltpu.VMEM((4, SPAN, 256), BF16),
            pltpu.VMEM((3, SPAN, 256), BF16),
            pltpu.SemaphoreType.DMA((3,)),
            pltpu.SemaphoreType.DMA((copies,)),
            pltpu.SemaphoreType.DMA((copies,)),
        ],
        compiler_params=pltpu.CompilerParams(
            collective_id=0, has_side_effects=True, vmem_limit_bytes=50 << 20
        ),
        name="attend_and_gather",
    )(lengths, prefixes, queries, new_kv, resid, kv_cache, out_weight)


def ffn_kernel(
    length_ref, gain_ref, h_ref, gate_hbm, up_hbm, down_hbm,
    out_ref,
    gw, uw, dw, xs, own_h, sq_out, sq_in,
    send_core, recv_core, keep, stage, recv_one, recv_two, hid,
    pa, ra_one, ra_two, qa, za, pb, zb, qb, rb_one, rb_two,
    local_sems, send_sems, recv_sems,
):
    me = Place()
    links = Links(send_sems, recv_sems)
    f, t, y, z, x, c = me.f, me.t, me.y, me.z, me.x, me.c
    load_g = pltpu.make_async_copy(gate_hbm, gw, local_sems.at[0])
    load_u = pltpu.make_async_copy(up_hbm, uw, local_sems.at[1])
    load_d = pltpu.make_async_copy(down_hbm, dw, local_sems.at[2])
    load_g.start()
    load_u.start()
    load_d.start()
    friends = [me.ffn((f + d) % 8) for d in range(1, 8)]
    friends += [me.at_y(me.ya), me.at_y(me.yb), me.at_z(1), me.at_z(-1)]
    greet(friends)

    gain = gain_ref[...].astype(F32)
    lane = lax.broadcasted_iota(jnp.int32, (SPAN, 128), 1)
    squares = jnp.zeros((SPAN, 128), F32)
    for g in range(8):
        row, side = g // 2, g % 2
        rows = jnp.concatenate(
            [h_ref[p, side * 4 + k, row] for k in range(4) for p in range(2)], axis=1
        ).astype(F32)
        squares = jnp.where(lane == g, jnp.sum(rows * rows, axis=1, keepdims=True), squares)
        xs[side, row] = (rows * gain).astype(BF16)
    mine = jnp.concatenate(
        [h_ref[p, me.zh * 4 + k, y] for k in range(4) for p in range(2)], axis=1
    )
    own_h[...] = mine.astype(F32)
    turned = jnp.transpose(jnp.concatenate([squares, jnp.zeros((32, 128), F32)], axis=0))
    for g in range(8):
        sq_out[g] = jnp.broadcast_to(turned[g : g + 1], (8, 128))

    greeted(friends)
    sq_waits = []
    for d in range(1, 8):
        to = (f + d) % 8
        sq_waits.append(links.start(sq_out.at[to], sq_in.at[d - 1], me.ffn(to)))

    load_g.wait()
    load_u.wait()
    tail = jnp.zeros((4, 2, 48, 128), F32)

    def project(side, dst):
        rows = xs[side].reshape(4 * SPAN, WIDTH)
        for k, w in enumerate((gw, uw)):
            base = k * WIDTH
            dst[:, :, :, base + 896 : base + 1024] = tail.astype(dst.dtype)
            out = jnp.dot(rows, w[...], preferred_element_type=F32)
            dst[:, :, :, base : base + HID] = out.astype(dst.dtype).reshape(4, 2, 48, HID)

    project(1 - c, send_core)
    core_waits = [
        links.start(send_core.at[i], recv_core.at[i], me.core()) for i in range(4)
    ]
    project(c, keep)
    arrived(*core_waits)

    def joined(i, half):
        return keep[i, half] + recv_core[i, half].astype(F32)

    def push(half, blocks, device):
        waits = []
        for slot, i in enumerate(blocks):
            stage[i, half] = joined(i, half).astype(BF16)
            waits.append(links.start(stage.at[i, half], recv_one.at[half, slot], device))
        return waits

    wait_a = push(0, (me.xa, 3 - me.xa), me.at_x(me.xa))
    wait_b = push(1, (me.xb, flip(me.xb)), me.at_x(me.xb))
    arrived(*wait_a)
    stage[me.xb, 0] = (joined(me.xb, 0) + recv_one[0, 1].astype(F32)).astype(BF16)
    two_a = links.start(stage.at[me.xb, 0], recv_two.at[0], me.at_x(me.xb))
    arrived(*wait_b)
    stage[me.xa, 1] = (joined(me.xa, 1) + recv_one[1, 1].astype(F32)).astype(BF16)
    two_b = links.start(stage.at[me.xa, 1], recv_two.at[1], me.at_x(me.xa))

    arrived(*sq_waits)
    total = sq_out[f]
    for d in range(7):
        total += sq_in[d]
    total = jnp.transpose(jnp.concatenate([total] * 16, axis=0))
    rs = lax.rsqrt(total / D + 1e-06)[:SPAN, 0:1]

    def activate(half):
        both = (
            joined(x, half) + recv_one[half, 0].astype(F32) + recv_two[half].astype(F32)
        )
        r = rs[half * 48 : (half + 1) * 48]
        gate, up = both[:, :WIDTH] * r, both[:, WIDTH:] * r
        hid[c, x, half] = (gate / (1.0 + jnp.exp(-gate)) * up).astype(BF16)

    def share(where, device):
        return links.start(hid.at[where], hid.at[where], device)

    arrived(two_a)
    activate(0)
    one_a = share((c, x, 0), me.at_x(me.xa))
    core_waits = [share((c, x, 0), me.core())]
    arrived(two_b)
    activate(1)
    one_b = share((c, x, 1), me.at_x(me.xb))
    core_waits.append(share((c, x, 1), me.core()))
    arrived(one_a)
    x_pair = pl.ds(2 * (x // 2), 2)
    two_a = share((c, x_pair, 0), me.at_x(me.xb))
    core_waits.append(share((c, me.xa, 0), me.core()))
    arrived(one_b)
    two_b = share((c, x, 1), me.at_x(me.xa))
    two_c = share((c, me.xb, 1), me.at_x(me.xa))
    core_waits.append(share((c, me.xb, 1), me.core()))
    arrived(two_a)
    far_pair = pl.ds(2 - 2 * (x // 2), 2)
    core_waits.append(share((c, far_pair, 0), me.core()))
    arrived(two_b, two_c)
    core_waits.append(share((c, me.xa, 1), me.core()))
    core_waits.append(share((c, flip(me.xb), 1), me.core()))

    load_d.wait()

    def lower(side):
        rows = hid[side].reshape(4 * SPAN, WIDTH)[:, :HID]
        out = jnp.dot(rows, dw[...], preferred_element_type=F32)
        for i in range(4):
            for k in range(4):
                base = i * SPAN + k * ROWS_OUT
                piece = out[base : base + ROWS_OUT].astype(BF16)
                for j in range(2):
                    pa[j, i, side * 4 + k] = piece[:, j * 256 : (j + 1) * 256]
                    pb[side * 4 + k, j, i] = piece[:, 512 + j * 256 : 768 + j * 256]

    lower(c)
    arrived(*core_waits)
    lower(1 - c)

    def plus(*parts):
        out = parts[0].astype(F32)
        for part in parts[1:]:
            out += part.astype(F32)
        return out

    def y_stage(src, one, two):
        wait = [[], []]
        for slot, i in enumerate((me.ya, 3 - me.ya)):
            wait[0].append(links.start(src.at[0, i], one.at[0, slot], me.at_y(me.ya)))
        for slot, i in enumerate((me.yb, flip(me.yb))):
            wait[1].append(links.start(src.at[1, i], one.at[1, slot], me.at_y(me.yb)))
        yield
        yield
        arrived(*wait[0])
        src[0, me.yb] = plus(src[0, me.yb], one[0, 1]).astype(BF16)
        a = links.start(src.at[0, me.yb], two.at[0], me.at_y(me.yb))
        arrived(*wait[1])
        src[1, me.ya] = plus(src[1, me.ya], one[1, 1]).astype(BF16)
        b = links.start(src.at[1, me.ya], two.at[1], me.at_y(me.ya))
        yield
        arrived(a, b)

    def z_stage(src, got):
        far = (z + 4) % 8
        right = links.start(src.at[far, 0], got.at[0, 0, 0], me.at_z(1))
        left = links.start(src.at[far, 1], got.at[1, 0, 1], me.at_z(-1))
        yield
        for s in (1, 2, 3):
            at = (z + 4 - s) % 8
            arrived(right)
            if s == 1:
                src[at, 0] = plus(src[at, 0], got[0, 0, 0]).astype(BF16)
            else:
                src[at] = plus(src[at], got[0, s - 1]).astype(BF16)
            right = links.start(src.at[at], got.at[0, s], me.at_z(1))
            at = (z + 4 + s) % 8
            arrived(left)
            if s == 1:
                src[at, 1] = plus(src[at, 1], got[1, 0, 1]).astype(BF16)
            else:
                src[at] = plus(src[at], got[1, s - 1]).astype(BF16)
            left = links.start(src.at[at], got.at[1, s], me.at_z(-1))
            yield
        arrived(right, left)

    def y_first():
        yield from y_stage(pa, ra_one, ra_two)
        for j in range(2):
            qa[:, j] = plus(pa[j, y], ra_one[j, 0], ra_two[j]).astype(BF16)
        yield from z_stage(qa, za)

    def z_first():
        yield from z_stage(pb, zb)
        qb[...] = plus(pb[z], zb[0, 3], zb[1, 3]).astype(BF16)
        yield from y_stage(qb, rb_one, rb_two)

    in_turn(y_first(), z_first())
    left = plus(qa[z], za[0, 3], za[1, 3])
    right = [plus(qb[j, y], rb_one[j, 0], rb_two[j]) for j in range(2)]
    down = jnp.concatenate([left[0], left[1], right[0], right[1]], axis=1)
    start = pl.multiple_of(t * ROWS_OUT, 8)
    out = own_h[pl.ds(start, ROWS_OUT), :] + down
    live = start + lax.broadcasted_iota(jnp.int32, (ROWS_OUT, WIDTH), 0) < length_ref[0]
    out_ref[...] = jnp.where(live, out, 0.0).astype(BF16)
    links.finish()


def ffn_call(lengths, gain, h, gate_weight, up_weight, down_weight):
    vmem = pl.BlockSpec(memory_space=pltpu.VMEM)
    smem = pl.BlockSpec(memory_space=pltpu.SMEM)
    hbm = pl.BlockSpec(memory_space=pl.ANY)
    copies = 7 + 4 + 4 + 2 + 2 + 3 + 7 + 2 * 6 + 2 * 8
    piece = (ROWS_OUT, 256)
    return pl.pallas_call(
        ffn_kernel,
        out_shape=jax.ShapeDtypeStruct((ROWS_OUT, WIDTH), BF16),
        in_specs=[smem, vmem, vmem, hbm, hbm, hbm],
        out_specs=vmem,
        scratch_shapes=[
            pltpu.VMEM((WIDTH, HID), BF16),
            pltpu.VMEM((WIDTH, HID), BF16),
            pltpu.VMEM((HID, WIDTH), BF16),
            pltpu.VMEM((2, 4, SPAN, WIDTH), BF16),
            pltpu.VMEM((SPAN, WIDTH), F32),
            pltpu.VMEM((8, 8, 128), F32),
            pltpu.VMEM((7, 8, 128), F32),
            pltpu.VMEM((4, 2, 48, 2 * WIDTH), BF16),
            pltpu.VMEM((4, 2, 48, 2 * WIDTH), BF16),
            pltpu.VMEM((4, 2, 48, 2 * WIDTH), F32),
            pltpu.VMEM((4, 2, 48, 2 * WIDTH), BF16),
            pltpu.VMEM((2, 2, 48, 2 * WIDTH), BF16),
            pltpu.VMEM((2, 48, 2 * WIDTH), BF16),
            pltpu.VMEM((2, 4, 2, 48, WIDTH), BF16),
            pltpu.VMEM((2, 4, 8) + piece, BF16),
            pltpu.VMEM((2, 2, 8) + piece, BF16),
            pltpu.VMEM((2, 8) + piece, BF16),
            pltpu.VMEM((8, 2) + piece, BF16),
            pltpu.VMEM((2, 4, 2) + piece, BF16),
            pltpu.VMEM((8, 2, 4) + piece, BF16),
            pltpu.VMEM((2, 4, 2, 4) + piece, BF16),
            pltpu.VMEM((2, 4) + piece, BF16),
            pltpu.VMEM((2, 2) + piece, BF16),
            pltpu.VMEM((2,) + piece, BF16),
            pltpu.SemaphoreType.DMA((3,)),
            pltpu.SemaphoreType.DMA((copies,)),
            pltpu.SemaphoreType.DMA((copies,)),
        ],
        compiler_params=pltpu.CompilerParams(
            collective_id=1, has_side_effects=True, vmem_limit_bytes=56 << 20
        ),
        name="feed_forward",
    )(lengths, gain, h, gate_weight, up_weight, down_weight)


def body(
    queries,
    new_kv,
    kv_cache,
    lengths,
    prefixes,
    resid,
    out_weight,
    gain,
    gate_weight,
    up_weight,
    down_weight,
):
    h = attention_call(lengths, prefixes, queries, new_kv, resid, kv_cache, out_weight)
    return ffn_call(lengths, gain.reshape(1, -1), h, gate_weight, up_weight, down_weight)


def solution(mesh):
    return jax.shard_map(
        body,
        mesh=mesh,
        in_specs=(
            P("grp", "tp"),
            P(None, "grp", "tp"),
            P(None, "grp", "ffn", "tp"),
            P("grp"),
            P("grp"),
            P("grp", "ffn"),
            P("tp", "ffn"),
            P("ffn"),
            P("ffn", ("grp", "tp")),
            P("ffn", ("grp", "tp")),
            P(("grp", "tp"), "ffn"),
        ),
        out_specs=P(("grp", "tp"), "ffn"),
        check_vma=False,
    )
```

```python
import functools
import math

import jax
import jax.numpy as jnp
from jax import lax
from jax.experimental import pallas as pl
from jax.experimental.pallas import tpu as pltpu
from jax.sharding import PartitionSpec as P

MESH = pl.DeviceIdType.MESH
F32 = jnp.float32
BF16 = jnp.bfloat16

D = 8192
DH = 128
SPAN = 96
ROWS_OUT = 24
MAIN = 896
REST = 28
BOTH = 1920
KEYS = 2048
WIDTH = 1024
HID = 924
NEG = -1e30
SCALE = math.log2(math.e) / math.sqrt(DH)


class Place:
    def __init__(self):
        g = lax.axis_index("grp")
        self.t = lax.axis_index("tp")
        self.f = lax.axis_index("ffn")
        self.y, self.zh = g // 2, g % 2
        self.x, self.c = self.f // 2, self.f % 2
        self.z = self.zh * 4 + self.t
        self.xa, self.xb = flip(self.x), 3 - self.x
        self.ya, self.yb = flip(self.y), 3 - self.y

    def ffn(self, f):
        return {"ffn": f}

    def tp(self, t):
        return {"tp": t}

    def core(self):
        return {"ffn": self.x * 2 + 1 - self.c}

    def at_x(self, x):
        return {"ffn": x * 2 + self.c}

    def at_y(self, y):
        return {"grp": y * 2 + self.zh}

    def at_y_step(self, step):
        return self.at_y((self.y + step) % 4)

    def at_z(self, step):
        z = (self.z + step + 8) % 8
        return {"grp": self.y * 2 + z // 4, "tp": z % 4}


def flip(v):
    return v + 1 - 2 * (v % 2)


class Links:
    def __init__(self, send_sems, recv_sems):
        self.send_sems, self.recv_sems = send_sems, recv_sems
        self.started = []

    def start(self, src, dst, device):
        k = len(self.started)
        copy = pltpu.make_async_remote_copy(
            src_ref=src,
            dst_ref=dst,
            send_sem=self.send_sems.at[k],
            recv_sem=self.recv_sems.at[k],
            device_id=device,
            device_id_type=MESH,
        )
        copy.start()
        self.started.append(copy)
        return copy

    def finish(self):
        for copy in self.started:
            copy.wait_send()


def greet(devices):
    barrier = pltpu.get_barrier_semaphore()
    for device in devices:
        pl.semaphore_signal(barrier, inc=1, device_id=device, device_id_type=MESH)


def greeted(devices):
    pl.semaphore_wait(pltpu.get_barrier_semaphore(), len(devices))


def in_turn(*flows):
    alive = list(flows)
    while alive:
        for flow in list(alive):
            try:
                next(flow)
            except StopIteration:
                alive.remove(flow)


def arrived(*copies):
    for copy in copies:
        copy.wait_recv()


NT = (((1,), (1,)), ((), ()))


def plus(*parts):
    out = parts[0].astype(F32)
    for part in parts[1:]:
        out += part.astype(F32)
    return out


def layer_kernel(
    length_ref, prefix_ref, gain_ref,
    q_hbm, new_hbm, resid_hbm, cache_hbm, wo_hbm, gate_hbm, up_hbm, down_hbm,
    out_ref,
    q_ref, new_ref, resid_ref, kv, wo, gw, uw, rw, dw,
    o_out, st_out, o_in, st_in, att, part_f, part_b, part_in, h_ref,
    xs, own_h, sq_out, sq_in,
    send_core, recv_core, keep, stage, recv_one, recv_two, hid,
    pieces, from_y, summed, za, zb, done, last,
    local_sems, send_sems, recv_sems,
):
    me = Place()
    links = Links(send_sems, recv_sems)
    f, t, y, z, x, c = me.f, me.t, me.y, me.z, me.x, me.c

    def load(k, src, dst):
        copy = pltpu.make_async_copy(src, dst, local_sems.at[k])
        copy.start()
        return copy

    first = [
        load(0, q_hbm, q_ref),
        load(1, cache_hbm.at[0, 0], kv.at[0]),
        load(2, new_hbm, new_ref),
        load(3, cache_hbm.at[1, 0], kv.at[1]),
    ]
    friends = [me.ffn((f + d) % 8) for d in range(1, 8)]
    friends += [me.tp((t + d) % 4) for d in range(1, 4)]
    friends += [me.at_y_step(d) for d in range(1, 4)]
    friends += [me.at_z(1), me.at_z(-1)]
    greet(friends)

    length, prefix = length_ref[0], prefix_ref[0]
    lanes = lax.broadcasted_iota(jnp.int32, (1, KEYS), 1)
    bias = jnp.where(f * KEYS + lanes < prefix, 0.0, NEG).astype(F32)
    slot = lax.broadcasted_iota(jnp.int32, (SPAN, SPAN), 0)
    key = lax.broadcasted_iota(jnp.int32, (SPAN, SPAN), 1)
    limit = jnp.where(f == 0, length, 0)
    new_bias = jnp.where((key <= slot) & (key < limit), 0.0, NEG).astype(F32)
    new_bias = jnp.concatenate([new_bias] * 4, axis=0)
    lane = lax.broadcasted_iota(jnp.int32, (4 * SPAN, 128), 1)
    for copy in first:
        copy.wait()
    load_wo = load(4, wo_hbm, wo)
    load_r = load(5, resid_hbm, resid_ref)
    load_g = load(6, gate_hbm, gw)
    load_u = load(7, up_hbm, uw)
    load_d = load(8, down_hbm, dw)

    def attend(step, carry):
        half, h = step // 2, step % 2
        cols = pl.ds(pl.multiple_of(h * DH, DH), DH)
        keys, values = kv[0, :, cols], kv[1, :, cols]
        new_keys, new_values = new_ref[0, :, cols], new_ref[1, :, cols]
        q = jnp.concatenate(
            [
                q_ref[:, pl.ds(pl.multiple_of((h * 8 + half * 4 + i) * DH, DH), DH)]
                for i in range(4)
            ],
            axis=0,
        )
        s = lax.dot_general(q, keys, NT, preferred_element_type=F32) + bias
        s_new = lax.dot_general(q, new_keys, NT, preferred_element_type=F32) + new_bias
        top = jnp.maximum(
            jnp.max(s, axis=1, keepdims=True), jnp.max(s_new, axis=1, keepdims=True)
        )
        p = jnp.exp2((s - top) * SCALE).astype(BF16)
        p_new = jnp.exp2((s_new - top) * SCALE).astype(BF16)
        wide = jnp.concatenate([values, jnp.ones((KEYS, DH), BF16)], axis=1)
        wide_new = jnp.concatenate([new_values, jnp.ones((SPAN, DH), BF16)], axis=1)
        acc = jnp.dot(p, wide, preferred_element_type=F32) + jnp.dot(
            p_new, wide_new, preferred_element_type=F32
        )
        total = acc[:, DH:]
        out = (acc[:, :DH] / total).astype(BF16)
        stats = jnp.where(lane == 0, top, jnp.where(lane == 1, total, 0.0))
        for i in range(4):
            rows = slice(i * SPAN, (i + 1) * SPAN)
            o_out[half * 4 + i, h] = out[rows]
            square = jnp.concatenate([stats[rows], jnp.zeros((32, 128), F32)], axis=0)
            st_out[half * 4 + i, h] = jnp.transpose(square)[:8]
        return carry

    lax.fori_loop(0, 4, attend, 0)

    greeted(friends)
    waits = []
    for d in range(1, 8):
        to = (f + d) % 8
        waits.append(links.start(st_out.at[to], st_in.at[d], me.ffn(to)))
        waits.append(links.start(o_out.at[to], o_in.at[d], me.ffn(to)))
    arrived(*waits)
    for h in range(2):
        stats = [st_out[f, h]] + [st_in[d, h] for d in range(1, 8)]
        tops = [s[0:1] for s in stats]
        top = functools.reduce(jnp.maximum, tops)
        weights = [s[1:2] * jnp.exp2((m - top) * SCALE) for s, m in zip(stats, tops)]
        total = sum(weights[1:], weights[0])
        shares = jnp.concatenate(
            [w / total for w in weights] + [jnp.zeros((120, 128), F32)], axis=0
        )
        shares = jnp.transpose(shares)[:SPAN]
        mine = o_out[f, h].astype(F32) * shares[:, 0:1]
        for d in range(1, 8):
            mine += o_in[d, h].astype(F32) * shares[:, d : d + 1]
        att[f, h] = mine.astype(BF16)
    waits = [links.start(att.at[f], att.at[f], me.ffn((f + d) % 8)) for d in range(1, 8)]

    load_wo.wait()
    load_r.wait()
    load_g.wait()
    load_u.wait()
    rw[...] = jnp.zeros((128, WIDTH), BF16)
    rw[0:REST] = gw[MAIN:HID]
    rw[64 : 64 + REST] = uw[MAIN:HID]
    arrived(*waits)
    attn = jnp.concatenate([att[q, h] for h in range(2) for q in range(8)], axis=1)
    part = jnp.dot(attn, wo[...], preferred_element_type=F32)
    for j in range(4):
        piece = part[:, j * 256 : (j + 1) * 256]
        part_f[j] = piece
        part_b[j] = piece.astype(BF16)
    waits = []
    for d in range(1, 4):
        to = (t + d) % 4
        waits.append(links.start(part_b.at[to], part_in.at[d - 1], me.tp(to)))
    arrived(*waits)
    h1 = part_f[t] + resid_ref[:, pl.ds(pl.multiple_of(t * 256, 256), 256)].astype(F32)
    for d in range(3):
        h1 += part_in[d].astype(F32)
    h1 = h1.astype(BF16)
    h_ref[0, z, y] = h1[:, :128]
    h_ref[1, z, y] = h1[:, 128:]

    def pass_on(ref, device):
        return links.start(ref, ref, device)

    def ring(p, row, seen):
        right = pass_on(h_ref.at[p, z, row], me.at_z(1))
        left = pass_on(h_ref.at[p, z, row], me.at_z(-1))
        yield
        for s in (1, 2, 3):
            rows = (pl.ds(0, SPAN), pl.ds(0, SPAN)) if s < 3 else (pl.ds(0, 48), pl.ds(48, 48))
            at = (z - s + 8) % 8
            arrived(right)
            right = pass_on(h_ref.at[p, at, row, rows[0]], me.at_z(1))
            seen(at)
            at = (z + s) % 8
            arrived(left)
            left = pass_on(h_ref.at[p, at, row, rows[1]], me.at_z(-1))
            seen(at)
            yield
        arrived(right, left)
        seen((z + 4) % 8)

    def from_peer(d):
        copy = pass_on(h_ref.at[0, z, y], me.at_y_step(d))
        yield
        arrived(copy)
        yield from ring(0, (y + 4 - d) % 4, lambda at: None)

    def own_then_peers():
        waits = []

        def seen(at):
            for d in (1, 2, 3):
                waits.append(pass_on(h_ref.at[1, at, y], me.at_y_step(d)))

        seen(z)
        yield from ring(1, y, seen)
        yield
        arrived(*waits)

    in_turn(
        ring(0, y, lambda at: None),
        from_peer(1),
        from_peer(3),
        from_peer(2),
        own_then_peers(),
    )

    gain = gain_ref[...].astype(F32).reshape(1, WIDTH)
    lane = lax.broadcasted_iota(jnp.int32, (SPAN, 128), 1)
    squares = jnp.zeros((SPAN, 128), F32)

    def rows_of(side, row):
        return jnp.concatenate(
            [h_ref[p, side * 4 + k, row] for k in range(4) for p in range(2)], axis=1
        ).astype(F32)

    for g in range(8):
        rows = rows_of(g % 2, g // 2)
        squares = jnp.where(lane == g, jnp.sum(rows * rows, axis=1, keepdims=True), squares)
        xs[g % 2, g // 2] = (rows * gain).astype(BF16)

    def project(side, dst):
        rows = xs[side].reshape(4 * SPAN, WIDTH)
        for w, base, size in ((gw, 0, MAIN), (uw, MAIN, MAIN), (rw, 2 * MAIN, 128)):
            out = lax.dot_general(rows, w[0:size], NT, preferred_element_type=F32)
            dst[:, :, :, base : base + size] = out.astype(dst.dtype).reshape(4, 2, 48, size)

    project(1 - c, send_core)
    core_waits = [
        links.start(send_core.at[i], recv_core.at[i], me.core()) for i in range(4)
    ]
    turned = jnp.transpose(jnp.concatenate([squares, jnp.zeros((32, 128), F32)], axis=0))
    for g in range(8):
        sq_out[g] = jnp.broadcast_to(turned[g : g + 1], (8, 128))
    sq_waits = []
    for d in range(1, 8):
        to = (f + d) % 8
        sq_waits.append(links.start(sq_out.at[to], sq_in.at[d - 1], me.ffn(to)))
    project(c, keep)
    arrived(*core_waits)

    def joined(i, half):
        return keep[i, half] + recv_core[i, half].astype(F32)

    def push(half, slot, i, device):
        stage[i, half] = joined(i, half).astype(BF16)
        return links.start(stage.at[i, half], recv_one.at[half, slot], device)

    far_a = push(0, 1, 3 - me.xa, me.at_x(me.xa))
    far_b = push(1, 1, flip(me.xb), me.at_x(me.xb))
    near_a = push(0, 0, me.xa, me.at_x(me.xa))
    near_b = push(1, 0, me.xb, me.at_x(me.xb))
    own_h[...] = rows_of(me.zh, y)
    arrived(far_a)
    stage[me.xb, 0] = (joined(me.xb, 0) + recv_one[0, 1].astype(F32)).astype(BF16)
    two_a = links.start(stage.at[me.xb, 0], recv_two.at[0], me.at_x(me.xb))
    arrived(far_b)
    stage[me.xa, 1] = (joined(me.xa, 1) + recv_one[1, 1].astype(F32)).astype(BF16)
    two_b = links.start(stage.at[me.xa, 1], recv_two.at[1], me.at_x(me.xa))

    arrived(*sq_waits)
    total = sq_out[f]
    for d in range(7):
        total += sq_in[d]
    total = jnp.transpose(jnp.concatenate([total] * 16, axis=0))
    rs = lax.rsqrt(total / D + 1e-06)[:SPAN, 0:1]

    def silu(v):
        return v / (1.0 + jnp.exp(-v))

    def activate(half):
        both = plus(joined(x, half), recv_one[half, 0], recv_two[half])
        both = both * rs[half * 48 : (half + 1) * 48]
        rest = both[:, 2 * MAIN :]
        hid[c, x, half, :, 0:MAIN] = (silu(both[:, :MAIN]) * both[:, MAIN : 2 * MAIN]).astype(BF16)
        hid[c, x, half, :, MAIN:] = (silu(rest) * pltpu.roll(rest, 64, 1)).astype(BF16)

    def share(half, i, device):
        return pass_on(hid.at[c, i, half], device)

    arrived(near_a, two_a)
    activate(0)
    a0 = share(0, x, me.at_x(me.xa))
    b0 = share(0, x, me.at_x(me.xb))
    core_waits = [share(0, x, me.core())]
    arrived(near_b, two_b)
    activate(1)
    b1 = share(1, x, me.at_x(me.xb))
    a1 = share(1, x, me.at_x(me.xa))
    core_waits.append(share(1, x, me.core()))
    arrived(a0)
    far_0 = share(0, me.xa, me.at_x(me.xb))
    core_waits.append(share(0, me.xa, me.core()))
    arrived(b1)
    far_1 = share(1, me.xb, me.at_x(me.xa))
    core_waits.append(share(1, me.xb, me.core()))
    arrived(b0)
    core_waits.append(share(0, me.xb, me.core()))
    arrived(a1)
    core_waits.append(share(1, me.xa, me.core()))
    load_d.wait()
    arrived(far_0)
    core_waits.append(share(0, flip(me.xb), me.core()))
    arrived(far_1)
    core_waits.append(share(1, flip(me.xb), me.core()))

    def lower(side):
        rows = hid[side].reshape(4 * SPAN, WIDTH)[:, :HID]
        out = jnp.dot(rows, dw[...], preferred_element_type=F32)
        for i in range(4):
            for k in range(4):
                base = i * SPAN + k * ROWS_OUT
                piece = out[base : base + ROWS_OUT].astype(BF16)
                for j in range(4):
                    pieces[j // 2, side * 4 + k, i, j % 2] = piece[:, j * 256 : (j + 1) * 256]

    lower(c)
    arrived(*core_waits)
    lower(1 - c)

    def z_stage(src, got):
        far = (z + 4) % 8
        right = links.start(src(far).at[0], got.at[0, 0, 0], me.at_z(1))
        left = links.start(src(far).at[1], got.at[1, 0, 1], me.at_z(-1))
        yield
        for s in (1, 2, 3):
            for way, at in ((0, (z + 4 - s) % 8), (1, (z + 4 + s) % 8)):
                ref = src(at)
                arrived(left if way else right)
                if s == 1:
                    ref[way] = plus(ref[way], got[way, 0, way]).astype(BF16)
                else:
                    ref[...] = plus(ref[...], got[way, s - 1]).astype(BF16)
                if way:
                    left = links.start(ref, got.at[1, s], me.at_z(-1))
                else:
                    right = links.start(ref, got.at[0, s], me.at_z(1))
            yield
        arrived(right, left)

    def y_first():
        waits = {}
        for s in (4, 3, 5, 2, 6, 1, 7, 0):
            at = (z + s) % 8
            waits[s] = [
                links.start(
                    pieces.at[0, at, (y + d) % 4], from_y.at[d - 1, at], me.at_y_step(d)
                )
                for d in (1, 3, 2)
            ]
        yield
        ready = set()

        def src(at_step):
            at = (z + at_step) % 8
            if at_step not in ready:
                arrived(*waits[at_step])
                summed[at] = plus(
                    pieces[0, at, y], from_y[0, at], from_y[1, at], from_y[2, at]
                ).astype(BF16)
                ready.add(at_step)
            return summed.at[at]

        far = src(4)
        right = links.start(far.at[0], za.at[0, 0, 0], me.at_z(1))
        left = links.start(far.at[1], za.at[1, 0, 1], me.at_z(-1))
        src(3)
        src(5)
        yield
        for s in (1, 2, 3):
            for way, step in ((0, 4 - s), (1, 4 + s)):
                ref = src(step)
                arrived(left if way else right)
                if s == 1:
                    ref[way] = plus(ref[way], za[way, 0, way]).astype(BF16)
                else:
                    ref[...] = plus(ref[...], za[way, s - 1]).astype(BF16)
                if way:
                    left = links.start(ref, za.at[1, s], me.at_z(-1))
                else:
                    right = links.start(ref, za.at[0, s], me.at_z(1))
            yield
        src(0)
        arrived(right, left)

    def z_first(d):
        row = (y + d) % 4
        got = zb.at[d]
        yield from z_stage(lambda at: pieces.at[1, at, row], got)
        if d:
            done[d - 1] = plus(pieces[1, z, row], got[0, 3], got[1, 3]).astype(BF16)
            copy = links.start(done.at[d - 1], last.at[d - 1], me.at_y_step(d))
            yield
            arrived(copy)

    in_turn(y_first(), z_first(2), z_first(1), z_first(3), z_first(0))
    left = plus(summed[z], za[0, 3], za[1, 3])
    right = plus(pieces[1, z, y], zb[0, 0, 3], zb[0, 1, 3], last[0], last[1], last[2])
    down = jnp.concatenate([left[0], left[1], right[0], right[1]], axis=1)
    start = pl.multiple_of(t * ROWS_OUT, 8)
    out = own_h[pl.ds(start, ROWS_OUT), :] + down
    live = start + lax.broadcasted_iota(jnp.int32, (ROWS_OUT, WIDTH), 0) < length
    out_ref[...] = jnp.where(live, out, 0.0).astype(BF16)
    links.finish()


def layer_call(*args):
    vmem = pl.BlockSpec(memory_space=pltpu.VMEM)
    smem = pl.BlockSpec(memory_space=pltpu.SMEM)
    hbm = pl.BlockSpec(memory_space=pl.ANY)
    copies = 14 + 7 + 3 + 40 + 3 + 24 + 4 + 7 + 6 + 14 + 24 + 8 + 32 + 3
    piece = (2, ROWS_OUT, 256)
    block = (4, 2, 48, BOTH)
    return pl.pallas_call(
        layer_kernel,
        out_shape=jax.ShapeDtypeStruct((ROWS_OUT, WIDTH), BF16),
        in_specs=[smem, smem, vmem] + [hbm] * 8,
        out_specs=vmem,
        scratch_shapes=[
            pltpu.VMEM((SPAN, 2048), BF16),
            pltpu.VMEM((2, SPAN, 256), BF16),
            pltpu.VMEM((SPAN, WIDTH), BF16),
            pltpu.VMEM((2, KEYS, 256), BF16),
            pltpu.VMEM((2048, WIDTH), BF16),
            pltpu.VMEM((HID, WIDTH), BF16),
            pltpu.VMEM((HID, WIDTH), BF16),
            pltpu.VMEM((128, WIDTH), BF16),
            pltpu.VMEM((HID, WIDTH), BF16),
            pltpu.VMEM((8, 2, SPAN, DH), BF16),
            pltpu.VMEM((8, 2, 8, 128), F32),
            pltpu.VMEM((8, 2, SPAN, DH), BF16),
            pltpu.VMEM((8, 2, 8, 128), F32),
            pltpu.VMEM((8, 2, SPAN, DH), BF16),
            pltpu.VMEM((4, SPAN, 256), F32),
            pltpu.VMEM((4, SPAN, 256), BF16),
            pltpu.VMEM((3, SPAN, 256), BF16),
            pltpu.VMEM((2, 8, 4, SPAN, 128), BF16),
            pltpu.VMEM((2, 4, SPAN, WIDTH), BF16),
            pltpu.VMEM((SPAN, WIDTH), F32),
            pltpu.VMEM((8, 8, 128), F32),
            pltpu.VMEM((7, 8, 128), F32),
            pltpu.VMEM(block, BF16),
            pltpu.VMEM(block, BF16),
            pltpu.VMEM(block, F32),
            pltpu.VMEM(block, BF16),
            pltpu.VMEM((2, 2, 48, BOTH), BF16),
            pltpu.VMEM((2, 48, BOTH), BF16),
            pltpu.VMEM((2, 4, 2, 48, WIDTH), BF16),
            pltpu.VMEM((2, 8, 4) + piece, BF16),
            pltpu.VMEM((3, 8) + piece, BF16),
            pltpu.VMEM((8,) + piece, BF16),
            pltpu.VMEM((2, 4) + piece, BF16),
            pltpu.VMEM((4, 2, 4) + piece, BF16),
            pltpu.VMEM((3,) + piece, BF16),
            pltpu.VMEM((3,) + piece, BF16),
            pltpu.SemaphoreType.DMA((9,)),
            pltpu.SemaphoreType.DMA((copies,)),
            pltpu.SemaphoreType.DMA((copies,)),
        ],
        compiler_params=pltpu.CompilerParams(
            collective_id=0, has_side_effects=True, vmem_limit_bytes=60 << 20
        ),
        name="layer",
    )(*args)


def body(
    queries,
    new_kv,
    kv_cache,
    lengths,
    prefixes,
    resid,
    out_weight,
    gain,
    gate_weight,
    up_weight,
    down_weight,
):
    return layer_call(
        lengths,
        prefixes,
        gain,
        queries,
        new_kv,
        resid,
        kv_cache,
        out_weight,
        gate_weight.T,
        up_weight.T,
        down_weight,
    )


def solution(mesh):
    return jax.shard_map(
        body,
        mesh=mesh,
        in_specs=(
            P("grp", "tp"),
            P(None, "grp", "tp"),
            P(None, "grp", "ffn", "tp"),
            P("grp"),
            P("grp"),
            P("grp", "ffn"),
            P("tp", "ffn"),
            P("ffn"),
            P("ffn", ("grp", "tp")),
            P("ffn", ("grp", "tp")),
            P(("grp", "tp"), "ffn"),
        ),
        out_specs=P(("grp", "tp"), "ffn"),
        check_vma=False,
    )
```

```python
import functools
import math

import jax
import jax.numpy as jnp
from jax import lax
from jax.experimental import pallas as pl
from jax.experimental.pallas import tpu as pltpu
from jax.sharding import PartitionSpec as P

MESH = pl.DeviceIdType.MESH
F32 = jnp.float32
BF16 = jnp.bfloat16

D = 8192
DH = 128
SPAN = 96
ROWS_OUT = 24
MAIN = 896
REST = 28
BOTH = 1920
KEYS = 2048
WIDTH = 1024
HID = 924
NEG = -1e30
SCALE = math.log2(math.e) / math.sqrt(DH)


class Place:
    def __init__(self):
        g = lax.axis_index("grp")
        self.t = lax.axis_index("tp")
        self.f = lax.axis_index("ffn")
        self.y, self.zh = g // 2, g % 2
        self.x, self.c = self.f // 2, self.f % 2
        self.z = self.zh * 4 + self.t
        self.xa, self.xb = flip(self.x), 3 - self.x
        self.ya, self.yb = flip(self.y), 3 - self.y

    def ffn(self, f):
        return {"ffn": f}

    def tp(self, t):
        return {"tp": t}

    def core(self):
        return {"ffn": self.x * 2 + 1 - self.c}

    def at_x(self, x):
        return {"ffn": x * 2 + self.c}

    def at_y(self, y):
        return {"grp": y * 2 + self.zh}

    def at_y_step(self, step):
        return self.at_y((self.y + step) % 4)

    def at_z(self, step):
        z = (self.z + step + 8) % 8
        return {"grp": self.y * 2 + z // 4, "tp": z % 4}


def flip(v):
    return v + 1 - 2 * (v % 2)


class Links:
    def __init__(self, send_sems, recv_sems):
        self.send_sems, self.recv_sems = send_sems, recv_sems
        self.started = []

    def start(self, src, dst, device):
        copy = self.make(src, dst, device)
        copy.start()
        return copy

    def make(self, src, dst, device):
        k = len(self.started)
        copy = pltpu.make_async_remote_copy(
            src_ref=src,
            dst_ref=dst,
            send_sem=self.send_sems.at[k],
            recv_sem=self.recv_sems.at[k],
            device_id=device,
            device_id_type=MESH,
        )
        self.started.append(copy)
        return copy

    def finish(self):
        for copy in self.started:
            copy.wait_send()


def greet(devices):
    barrier = pltpu.get_barrier_semaphore()
    for device in devices:
        pl.semaphore_signal(barrier, inc=1, device_id=device, device_id_type=MESH)


def greeted(devices):
    pl.semaphore_wait(pltpu.get_barrier_semaphore(), len(devices))


def in_turn(*flows):
    alive = list(flows)
    while alive:
        for flow in list(alive):
            try:
                next(flow)
            except StopIteration:
                alive.remove(flow)


def arrived(*copies):
    for copy in copies:
        copy.wait_recv()


NT = (((1,), (1,)), ((), ()))


def plus(*parts):
    out = parts[0].astype(F32)
    for part in parts[1:]:
        out += part.astype(F32)
    return out


def layer_kernel(
    length_ref, prefix_ref, gain_ref,
    q_hbm, new_hbm, resid_hbm, cache_hbm, wo_hbm, gate_hbm, up_hbm, down_hbm,
    out_ref,
    q_ref, new_ref, resid_ref, kv, wo, gw, uw, rw, dw,
    o_out, st_out, o_in, st_in, att, part_f, part_b, part_in, h_ref,
    xs, own_h, sq_out, sq_in,
    send_core, recv_core, keep, stage, recv_one, recv_two, hid,
    pieces, from_y, summed, near, relay, halves, far, done, last,
    local_sems, send_sems, recv_sems,
):
    me = Place()
    links = Links(send_sems, recv_sems)
    f, t, y, z, x, c = me.f, me.t, me.y, me.z, me.x, me.c

    def load(k, src, dst):
        copy = pltpu.make_async_copy(src, dst, local_sems.at[k])
        copy.start()
        return copy

    first = [
        load(0, q_hbm, q_ref),
        load(1, cache_hbm.at[0, 0], kv.at[0]),
        load(2, new_hbm, new_ref),
        load(3, cache_hbm.at[1, 0], kv.at[1]),
    ]
    friends = [me.ffn((f + d) % 8) for d in range(1, 8)]
    friends += [me.tp((t + d) % 4) for d in range(1, 4)]
    friends += [me.at_y_step(d) for d in range(1, 4)]
    friends += [me.at_z(step) for step in (1, -1, 2, -2)]
    greet(friends)

    length, prefix = length_ref[0], prefix_ref[0]
    lanes = lax.broadcasted_iota(jnp.int32, (1, KEYS), 1)
    bias = jnp.where(f * KEYS + lanes < prefix, 0.0, NEG).astype(F32)
    slot = lax.broadcasted_iota(jnp.int32, (SPAN, SPAN), 0)
    key = lax.broadcasted_iota(jnp.int32, (SPAN, SPAN), 1)
    limit = jnp.where(f == 0, length, 0)
    new_bias = jnp.where((key <= slot) & (key < limit), 0.0, NEG).astype(F32)
    new_bias = jnp.concatenate([new_bias] * 4, axis=0)
    lane = lax.broadcasted_iota(jnp.int32, (4 * SPAN, 128), 1)
    for copy in first:
        copy.wait()
    load_wo = load(4, wo_hbm, wo)
    load_r = load(5, resid_hbm, resid_ref)
    load_g = load(6, gate_hbm, gw)
    load_u = load(7, up_hbm, uw)
    load_d = load(8, down_hbm, dw)

    def attend(half, h):
        cols = pl.ds(pl.multiple_of(h * DH, DH), DH)
        keys, values = kv[0, :, cols], kv[1, :, cols]
        new_keys, new_values = new_ref[0, :, cols], new_ref[1, :, cols]
        q = jnp.concatenate(
            [
                q_ref[:, pl.ds(pl.multiple_of((h * 8 + half * 4 + i) * DH, DH), DH)]
                for i in range(4)
            ],
            axis=0,
        )
        s = lax.dot_general(q, keys, NT, preferred_element_type=F32) + bias
        s_new = lax.dot_general(q, new_keys, NT, preferred_element_type=F32) + new_bias
        top = jnp.maximum(
            jnp.max(s, axis=1, keepdims=True), jnp.max(s_new, axis=1, keepdims=True)
        )
        p = jnp.exp2((s - top) * SCALE).astype(BF16)
        p_new = jnp.exp2((s_new - top) * SCALE).astype(BF16)
        wide = jnp.concatenate([values, jnp.ones((KEYS, DH), BF16)], axis=1)
        wide_new = jnp.concatenate([new_values, jnp.ones((SPAN, DH), BF16)], axis=1)
        acc = jnp.dot(p, wide, preferred_element_type=F32) + jnp.dot(
            p_new, wide_new, preferred_element_type=F32
        )
        total = acc[:, DH:]
        out = (acc[:, :DH] / total).astype(BF16)
        stats = jnp.where(lane == 0, top, jnp.where(lane == 1, total, 0.0))
        for i in range(4):
            rows = slice(i * SPAN, (i + 1) * SPAN)
            o_out[half * 4 + i, h] = out[rows]
            square = jnp.concatenate([stats[rows], jnp.zeros((32, 128), F32)], axis=0)
            st_out[half * 4 + i, h] = jnp.transpose(square)[:8]

    exchange = []
    for d in (2, 6, 3, 5, 4, 7, 1):
        to = (f + d) % 8
        exchange.append((to, links.make(st_out.at[to], st_in.at[d], me.ffn(to))))
        exchange.append((to, links.make(o_out.at[to], o_in.at[d], me.ffn(to))))
    for half in range(2):

        @pl.loop(0, 2)
        def _(h):
            attend(half, h)

        if half == 0:
            greeted(friends)
        for to, copy in exchange:
            pl.when(to // 4 == half)(copy.start)
    arrived(*[copy for to, copy in exchange])
    for h in range(2):
        stats = [st_out[f, h]] + [st_in[d, h] for d in range(1, 8)]
        tops = [s[0:1] for s in stats]
        top = functools.reduce(jnp.maximum, tops)
        weights = [s[1:2] * jnp.exp2((m - top) * SCALE) for s, m in zip(stats, tops)]
        total = sum(weights[1:], weights[0])
        shares = jnp.concatenate(
            [w / total for w in weights] + [jnp.zeros((120, 128), F32)], axis=0
        )
        shares = jnp.transpose(shares)[:SPAN]
        mine = o_out[f, h].astype(F32) * shares[:, 0:1]
        for d in range(1, 8):
            mine += o_in[d, h].astype(F32) * shares[:, d : d + 1]
        att[f, h] = mine.astype(BF16)
    waits = [links.start(att.at[f], att.at[f], me.ffn((f + d) % 8)) for d in range(1, 8)]

    load_wo.wait()
    load_r.wait()
    load_g.wait()
    load_u.wait()
    rw[...] = jnp.zeros((128, WIDTH), BF16)
    rw[0:REST] = gw[MAIN:HID]
    rw[64 : 64 + REST] = uw[MAIN:HID]
    arrived(*waits)
    attn = jnp.concatenate([att[q, h] for h in range(2) for q in range(8)], axis=1)
    part = jnp.dot(attn, wo[...], preferred_element_type=F32)
    for j in range(4):
        piece = part[:, j * 256 : (j + 1) * 256]
        part_f[j] = piece
        part_b[j] = piece.astype(BF16)
    waits = []
    for d in range(1, 4):
        to = (t + d) % 4
        waits.append(links.start(part_b.at[to], part_in.at[d - 1], me.tp(to)))
    arrived(*waits)
    h1 = part_f[t] + resid_ref[:, pl.ds(pl.multiple_of(t * 256, 256), 256)].astype(F32)
    for d in range(3):
        h1 += part_in[d].astype(F32)
    h1 = h1.astype(BF16)
    h_ref[z, y] = h1

    def pass_on(ref, device):
        return links.start(ref, ref, device)

    low, high = pl.ds(0, 48), pl.ds(48, 48)

    def along_z(row, seen):
        mine = h_ref.at[z, row]
        right2, left2 = pass_on(mine, me.at_z(2)), pass_on(mine, me.at_z(-2))
        right1, left1 = pass_on(mine, me.at_z(1)), pass_on(mine, me.at_z(-1))
        seen(z)
        yield
        at = (z + 6) % 8
        arrived(right2)
        right3 = pass_on(h_ref.at[at, row], me.at_z(1))
        right4 = pass_on(h_ref.at[at, row, low], me.at_z(2))
        far = (z + 2) % 8
        arrived(left2)
        left3 = pass_on(h_ref.at[far, row], me.at_z(-1))
        left4 = pass_on(h_ref.at[far, row, high], me.at_z(-2))
        arrived(right1)
        seen((z + 7) % 8)
        arrived(left1)
        seen((z + 1) % 8)
        seen(at)
        seen(far)
        yield
        arrived(right4, left4)
        seen((z + 4) % 8)
        arrived(right3)
        seen((z + 5) % 8)
        arrived(left3)
        seen((z + 3) % 8)

    def own_rows():
        waits = []

        def seen(at):
            for d in (1, 3):
                waits.append(pass_on(h_ref.at[at, y], me.at_y_step(d)))

        yield from along_z(y, seen)
        yield
        arrived(*waits)

    def opposite_rows():
        copy = pass_on(h_ref.at[z, y], me.at_y_step(2))
        yield
        arrived(copy)
        yield from along_z((y + 2) % 4, lambda at: None)

    in_turn(opposite_rows(), own_rows())

    gain = gain_ref[...].astype(F32).reshape(1, WIDTH)
    lane = lax.broadcasted_iota(jnp.int32, (SPAN, 128), 1)
    squares = jnp.zeros((SPAN, 128), F32)

    def rows_of(side, row):
        return jnp.concatenate(
            [h_ref[side * 4 + k, row] for k in range(4)], axis=1
        ).astype(F32)

    for g in range(8):
        rows = rows_of(g % 2, g // 2)
        squares = jnp.where(lane == g, jnp.sum(rows * rows, axis=1, keepdims=True), squares)
        xs[g % 2, g // 2] = (rows * gain).astype(BF16)

    def project(side, dst):
        rows = xs[side].reshape(4 * SPAN, WIDTH)
        for w, base, size in ((gw, 0, MAIN), (uw, MAIN, MAIN), (rw, 2 * MAIN, 128)):
            out = lax.dot_general(rows, w[0:size], NT, preferred_element_type=F32)
            dst[:, :, :, base : base + size] = out.astype(dst.dtype).reshape(4, 2, 48, size)

    project(1 - c, send_core)
    core_waits = [
        links.start(send_core.at[i], recv_core.at[i], me.core()) for i in range(4)
    ]
    turned = jnp.transpose(jnp.concatenate([squares, jnp.zeros((32, 128), F32)], axis=0))
    for g in range(8):
        sq_out[g] = jnp.broadcast_to(turned[g : g + 1], (8, 128))
    sq_waits = []
    for d in range(1, 8):
        to = (f + d) % 8
        sq_waits.append(links.start(sq_out.at[to], sq_in.at[d - 1], me.ffn(to)))
    project(c, keep)
    arrived(*core_waits)

    def joined(i, half):
        return keep[i, half] + recv_core[i, half].astype(F32)

    def push(half, slot, i, device):
        stage[i, half] = joined(i, half).astype(BF16)
        return links.start(stage.at[i, half], recv_one.at[half, slot], device)

    far_a = push(0, 1, 3 - me.xa, me.at_x(me.xa))
    far_b = push(1, 1, flip(me.xb), me.at_x(me.xb))
    near_a = push(0, 0, me.xa, me.at_x(me.xa))
    near_b = push(1, 0, me.xb, me.at_x(me.xb))
    own_h[...] = rows_of(me.zh, y)
    arrived(far_a)
    stage[me.xb, 0] = (joined(me.xb, 0) + recv_one[0, 1].astype(F32)).astype(BF16)
    two_a = links.start(stage.at[me.xb, 0], recv_two.at[0], me.at_x(me.xb))
    arrived(far_b)
    stage[me.xa, 1] = (joined(me.xa, 1) + recv_one[1, 1].astype(F32)).astype(BF16)
    two_b = links.start(stage.at[me.xa, 1], recv_two.at[1], me.at_x(me.xa))

    arrived(*sq_waits)
    total = sq_out[f]
    for d in range(7):
        total += sq_in[d]
    total = jnp.transpose(jnp.concatenate([total] * 16, axis=0))
    rs = lax.rsqrt(total / D + 1e-06)[:SPAN, 0:1]

    def silu(v):
        return v / (1.0 + jnp.exp(-v))

    def activate(half):
        both = plus(joined(x, half), recv_one[half, 0], recv_two[half])
        both = both * rs[half * 48 : (half + 1) * 48]
        rest = both[:, 2 * MAIN :]
        hid[c, x, half, :, 0:MAIN] = (silu(both[:, :MAIN]) * both[:, MAIN : 2 * MAIN]).astype(BF16)
        hid[c, x, half, :, MAIN:] = (silu(rest) * pltpu.roll(rest, 64, 1)).astype(BF16)

    def share(half, i, device):
        return pass_on(hid.at[c, i, half], device)

    arrived(near_a, two_a)
    activate(0)
    a0 = share(0, x, me.at_x(me.xa))
    b0 = share(0, x, me.at_x(me.xb))
    core_waits = [share(0, x, me.core())]
    arrived(near_b, two_b)
    activate(1)
    b1 = share(1, x, me.at_x(me.xb))
    a1 = share(1, x, me.at_x(me.xa))
    core_waits.append(share(1, x, me.core()))
    arrived(a0)
    far_0 = share(0, me.xa, me.at_x(me.xb))
    core_waits.append(share(0, me.xa, me.core()))
    arrived(b1)
    far_1 = share(1, me.xb, me.at_x(me.xa))
    core_waits.append(share(1, me.xb, me.core()))
    arrived(b0)
    core_waits.append(share(0, me.xb, me.core()))
    arrived(a1)
    core_waits.append(share(1, me.xa, me.core()))
    load_d.wait()
    arrived(far_0)
    core_waits.append(share(0, flip(me.xb), me.core()))
    arrived(far_1)
    core_waits.append(share(1, flip(me.xb), me.core()))

    def lower(side):
        rows = hid[side].reshape(4 * SPAN, WIDTH)[:, :HID]
        out = jnp.dot(rows, dw[...], preferred_element_type=F32)
        for i in range(4):
            for k in range(4):
                base = i * SPAN + k * ROWS_OUT
                piece = out[base : base + ROWS_OUT].astype(BF16)
                for j in range(2):
                    pieces[side * 4 + k, i, j] = piece[:, j * 512 : (j + 1) * 512]

    lower(c)
    arrived(*core_waits)
    lower(1 - c)

    def along_z_sum(src, near, relay, half, far):
        copies = []
        for way, sign in ((0, 1), (1, -1)):
            copies.append(
                (
                    links.start(src(3 * sign), relay.at[way], me.at_z(sign)),
                    links.start(src(4).at[way], half.at[way], me.at_z(2 * sign)),
                )
            )
        close = [
            links.start(src(sign), near.at[way], me.at_z(sign))
            for way, sign in ((0, 1), (1, -1))
        ]
        yield
        ends = []
        for way, sign in ((0, 1), (1, -1)):
            ref = src(2 * sign)
            arrived(*copies[way])
            ref[1 - way] = plus(ref[1 - way], relay[way, 1 - way]).astype(BF16)
            ref[way] = plus(ref[way], relay[way, way], half[way]).astype(BF16)
            ends.append(links.start(ref, far.at[way], me.at_z(2 * sign)))
        yield
        src(0)
        arrived(*close, *ends)

    def own_sum():
        waits = {}
        for s in (3, 5, 4, 1, 7, 2, 6, 0):
            at = (z + s) % 8
            waits[s] = [
                links.start(
                    pieces.at[at, (y + d) % 4], from_y.at[d // 2, at], me.at_y_step(d)
                )
                for d in (1, 3)
            ]
        yield

        def src(step):
            at = (z + step + 8) % 8
            if step % 8 in waits:
                arrived(*waits.pop(step % 8))
                summed[at] = plus(pieces[at, y], from_y[0, at], from_y[1, at]).astype(BF16)
            return summed.at[at]

        yield from along_z_sum(src, near.at[0], relay.at[0], halves.at[0], far.at[0])

    def opposite_sum():
        row = (y + 2) % 4
        yield from along_z_sum(
            lambda step: pieces.at[(z + step + 8) % 8, row],
            near.at[1], relay.at[1], halves.at[1], far.at[1],
        )
        done[...] = plus(
            pieces[z, row], near[1, 0], near[1, 1], far[1, 0], far[1, 1]
        ).astype(BF16)
        copy = links.start(done, last, me.at_y_step(2))
        yield
        arrived(copy)

    in_turn(opposite_sum(), own_sum())
    total = plus(summed[z], near[0, 0], near[0, 1], far[0, 0], far[0, 1], last[...])
    down = jnp.concatenate([total[0], total[1]], axis=1)
    start = pl.multiple_of(t * ROWS_OUT, 8)
    out = own_h[pl.ds(start, ROWS_OUT), :] + down
    live = start + lax.broadcasted_iota(jnp.int32, (ROWS_OUT, WIDTH), 0) < length
    out_ref[...] = jnp.where(live, out, 0.0).astype(BF16)
    links.finish()


def layer_call(*args):
    vmem = pl.BlockSpec(memory_space=pltpu.VMEM)
    smem = pl.BlockSpec(memory_space=pltpu.SMEM)
    hbm = pl.BlockSpec(memory_space=pl.ANY)
    copies = 14 + 7 + 3 + 33 + 4 + 7 + 6 + 14 + 33
    piece = (2, ROWS_OUT, 512)
    block = (4, 2, 48, BOTH)
    return pl.pallas_call(
        layer_kernel,
        out_shape=jax.ShapeDtypeStruct((ROWS_OUT, WIDTH), BF16),
        in_specs=[smem, smem, vmem] + [hbm] * 8,
        out_specs=vmem,
        scratch_shapes=[
            pltpu.VMEM((SPAN, 2048), BF16),
            pltpu.VMEM((2, SPAN, 256), BF16),
            pltpu.VMEM((SPAN, WIDTH), BF16),
            pltpu.VMEM((2, KEYS, 256), BF16),
            pltpu.VMEM((2048, WIDTH), BF16),
            pltpu.VMEM((HID, WIDTH), BF16),
            pltpu.VMEM((HID, WIDTH), BF16),
            pltpu.VMEM((128, WIDTH), BF16),
            pltpu.VMEM((HID, WIDTH), BF16),
            pltpu.VMEM((8, 2, SPAN, DH), BF16),
            pltpu.VMEM((8, 2, 8, 128), F32),
            pltpu.VMEM((8, 2, SPAN, DH), BF16),
            pltpu.VMEM((8, 2, 8, 128), F32),
            pltpu.VMEM((8, 2, SPAN, DH), BF16),
            pltpu.VMEM((4, SPAN, 256), F32),
            pltpu.VMEM((4, SPAN, 256), BF16),
            pltpu.VMEM((3, SPAN, 256), BF16),
            pltpu.VMEM((8, 4, SPAN, 256), BF16),
            pltpu.VMEM((2, 4, SPAN, WIDTH), BF16),
            pltpu.VMEM((SPAN, WIDTH), F32),
            pltpu.VMEM((8, 8, 128), F32),
            pltpu.VMEM((7, 8, 128), F32),
            pltpu.VMEM(block, BF16),
            pltpu.VMEM(block, BF16),
            pltpu.VMEM(block, F32),
            pltpu.VMEM(block, BF16),
            pltpu.VMEM((2, 2, 48, BOTH), BF16),
            pltpu.VMEM((2, 48, BOTH), BF16),
            pltpu.VMEM((2, 4, 2, 48, WIDTH), BF16),
            pltpu.VMEM((8, 4) + piece, BF16),
            pltpu.VMEM((2, 8) + piece, BF16),
            pltpu.VMEM((8,) + piece, BF16),
            pltpu.VMEM((2, 2) + piece, BF16),
            pltpu.VMEM((2, 2) + piece, BF16),
            pltpu.VMEM((2, 2, ROWS_OUT, 512), BF16),
            pltpu.VMEM((2, 2) + piece, BF16),
            pltpu.VMEM(piece, BF16),
            pltpu.VMEM(piece, BF16),
            pltpu.SemaphoreType.DMA((9,)),
            pltpu.SemaphoreType.DMA((copies,)),
            pltpu.SemaphoreType.DMA((copies,)),
        ],
        compiler_params=pltpu.CompilerParams(
            collective_id=0, has_side_effects=True, vmem_limit_bytes=60 << 20
        ),
        name="layer",
    )(*args)


def body(
    queries,
    new_kv,
    kv_cache,
    lengths,
    prefixes,
    resid,
    out_weight,
    gain,
    gate_weight,
    up_weight,
    down_weight,
):
    return layer_call(
        lengths,
        prefixes,
        gain,
        queries,
        new_kv,
        resid,
        kv_cache,
        out_weight,
        gate_weight.T,
        up_weight.T,
        down_weight,
    )


def solution(mesh):
    return jax.shard_map(
        body,
        mesh=mesh,
        in_specs=(
            P("grp", "tp"),
            P(None, "grp", "tp"),
            P(None, "grp", "ffn", "tp"),
            P("grp"),
            P("grp"),
            P("grp", "ffn"),
            P("tp", "ffn"),
            P("ffn"),
            P("ffn", ("grp", "tp")),
            P("ffn", ("grp", "tp")),
            P(("grp", "tp"), "ffn"),
        ),
        out_specs=P(("grp", "tp"), "ffn"),
        check_vma=False,
    )
```

```python
import functools
import math

import jax
import jax.numpy as jnp
from jax import lax
from jax.experimental import pallas as pl
from jax.experimental.pallas import tpu as pltpu
from jax.sharding import PartitionSpec as P

MESH = pl.DeviceIdType.MESH
F32 = jnp.float32
BF16 = jnp.bfloat16

D = 8192
DH = 128
SPAN = 96
ROWS_OUT = 24
QUERIES = 2
MAIN = 896
REST = 28
BOTH = 1920
KEYS = 2048
WIDTH = 1024
HID = 924
NEG = -1e30
SCALE = math.log2(math.e) / math.sqrt(DH)


class Place:
    def __init__(self):
        g = lax.axis_index("grp")
        self.t = lax.axis_index("tp")
        self.f = lax.axis_index("ffn")
        self.y, self.zh = g // 2, g % 2
        self.x, self.c = self.f // 2, self.f % 2
        self.z = self.zh * 4 + self.t
        self.xa, self.xb = flip(self.x), 3 - self.x
        self.ya, self.yb = flip(self.y), 3 - self.y

    def ffn(self, f):
        return {"ffn": f}

    def tp(self, t):
        return {"tp": t}

    def core(self):
        return {"ffn": self.x * 2 + 1 - self.c}

    def at_x(self, x):
        return {"ffn": x * 2 + self.c}

    def at_y(self, y):
        return {"grp": y * 2 + self.zh}

    def at_y_step(self, step):
        return self.at_y((self.y + step) % 4)

    def at_z(self, step):
        z = (self.z + step + 8) % 8
        return {"grp": self.y * 2 + z // 4, "tp": z % 4}


def flip(v):
    return v + 1 - 2 * (v % 2)


class Links:
    def __init__(self, send_sems, recv_sems):
        self.send_sems, self.recv_sems = send_sems, recv_sems
        self.started = []

    def start(self, src, dst, device):
        copy = self.make(src, dst, device)
        copy.start()
        return copy

    def make(self, src, dst, device):
        k = len(self.started)
        copy = pltpu.make_async_remote_copy(
            src_ref=src,
            dst_ref=dst,
            send_sem=self.send_sems.at[k],
            recv_sem=self.recv_sems.at[k],
            device_id=device,
            device_id_type=MESH,
        )
        self.started.append(copy)
        return copy

    def finish(self):
        for copy in self.started:
            copy.wait_send()


def greet(devices):
    barrier = pltpu.get_barrier_semaphore()
    for device in devices:
        pl.semaphore_signal(barrier, inc=1, device_id=device, device_id_type=MESH)


def greeted(devices):
    pl.semaphore_wait(pltpu.get_barrier_semaphore(), len(devices))


def in_turn(*flows):
    alive = list(flows)
    while alive:
        for flow in list(alive):
            try:
                next(flow)
            except StopIteration:
                alive.remove(flow)


def arrived(*copies):
    for copy in copies:
        copy.wait_recv()


NT = (((1,), (1,)), ((), ()))


def plus(*parts):
    out = parts[0].astype(F32)
    for part in parts[1:]:
        out += part.astype(F32)
    return out


def layer_kernel(
    length_ref, prefix_ref, gain_ref,
    q_hbm, new_hbm, resid_hbm, cache_hbm, wo_hbm, gate_hbm, up_hbm, down_hbm,
    out_ref,
    q_ref, new_ref, resid_ref, kv, wo, gw, uw, rw, dw,
    o_out, st_out, o_in, st_in, att, part_f, part_b, part_in, h_ref,
    xs, own_h, sq_out, sq_in,
    send_core, recv_core, keep, stage, recv_one, recv_two, hid,
    pieces, from_y, summed, near, relay, halves, far, done, last,
    local_sems, send_sems, recv_sems,
):
    me = Place()
    links = Links(send_sems, recv_sems)
    f, t, y, z, x, c = me.f, me.t, me.y, me.z, me.x, me.c

    def load(k, src, dst):
        copy = pltpu.make_async_copy(src, dst, local_sems.at[k])
        copy.start()
        return copy

    first = [
        load(0, q_hbm, q_ref),
        load(1, cache_hbm.at[0, 0], kv.at[0]),
        load(2, new_hbm, new_ref),
        load(3, cache_hbm.at[1, 0], kv.at[1]),
    ]
    friends = [me.ffn((f + d) % 8) for d in range(1, 8)]
    friends += [me.tp((t + d) % 4) for d in range(1, 4)]
    friends += [me.at_y_step(d) for d in range(1, 4)]
    friends += [me.at_z(step) for step in (1, -1, 2, -2)]
    greet(friends)

    length, prefix = length_ref[0], prefix_ref[0]
    lanes = lax.broadcasted_iota(jnp.int32, (1, KEYS), 1)
    bias = jnp.where(f * KEYS + lanes < prefix, 0.0, NEG).astype(F32)
    slot = lax.broadcasted_iota(jnp.int32, (SPAN, SPAN), 0)
    key = lax.broadcasted_iota(jnp.int32, (SPAN, SPAN), 1)
    limit = jnp.where(f == 0, length, 0)
    new_bias = jnp.where((key <= slot) & (key < limit), 0.0, NEG).astype(F32)
    new_bias = jnp.concatenate([new_bias] * QUERIES, axis=0)
    lane = lax.broadcasted_iota(jnp.int32, (QUERIES * SPAN, 128), 1)
    for copy in first:
        copy.wait()
    load_wo = load(4, wo_hbm, wo)
    load_r = load(5, resid_hbm, resid_ref)
    load_g = load(6, gate_hbm, gw)
    load_u = load(7, up_hbm, uw)
    load_d = load(8, down_hbm, dw)

    def attend(half, h):
        cols = pl.ds(pl.multiple_of(h * DH, DH), DH)
        keys, values = kv[0, :, cols], kv[1, :, cols]
        new_keys, new_values = new_ref[0, :, cols], new_ref[1, :, cols]
        wide = jnp.concatenate([values, jnp.ones((KEYS, DH), BF16)], axis=1)
        wide_new = jnp.concatenate([new_values, jnp.ones((SPAN, DH), BF16)], axis=1)
        for first_q in range(half * 4, half * 4 + 4, QUERIES):
            q = jnp.concatenate(
                [
                    q_ref[:, pl.ds(pl.multiple_of((h * 8 + first_q + i) * DH, DH), DH)]
                    for i in range(QUERIES)
                ],
                axis=0,
            )
            s = lax.dot_general(q, keys, NT, preferred_element_type=F32) + bias
            s_new = lax.dot_general(q, new_keys, NT, preferred_element_type=F32) + new_bias
            top = jnp.maximum(
                jnp.max(s, axis=1, keepdims=True), jnp.max(s_new, axis=1, keepdims=True)
            )
            p = jnp.exp2((s - top) * SCALE).astype(BF16)
            p_new = jnp.exp2((s_new - top) * SCALE).astype(BF16)
            acc = jnp.dot(p, wide, preferred_element_type=F32) + jnp.dot(
                p_new, wide_new, preferred_element_type=F32
            )
            total = acc[:, DH:]
            out = (acc[:, :DH] / total).astype(BF16)
            stats = jnp.where(lane == 0, top, jnp.where(lane == 1, total, 0.0))
            for i in range(QUERIES):
                rows = slice(i * SPAN, (i + 1) * SPAN)
                o_out[first_q + i, h] = out[rows]
                square = jnp.concatenate([stats[rows], jnp.zeros((32, 128), F32)], axis=0)
                st_out[first_q + i, h] = jnp.transpose(square)[:8]

    exchange = []
    for d in (2, 6, 3, 5, 4, 7, 1):
        to = (f + d) % 8
        exchange.append((to, links.make(st_out.at[to], st_in.at[d], me.ffn(to))))
        exchange.append((to, links.make(o_out.at[to], o_in.at[d], me.ffn(to))))
    for half in range(2):

        @pl.loop(0, 2)
        def _(h):
            attend(half, h)

        if half == 0:
            greeted(friends)
        for to, copy in exchange:
            pl.when(to // 4 == half)(copy.start)
    arrived(*[copy for to, copy in exchange])
    for h in range(2):
        stats = [st_out[f, h]] + [st_in[d, h] for d in range(1, 8)]
        tops = [s[0:1] for s in stats]
        top = functools.reduce(jnp.maximum, tops)
        weights = [s[1:2] * jnp.exp2((m - top) * SCALE) for s, m in zip(stats, tops)]
        total = sum(weights[1:], weights[0])
        shares = jnp.concatenate(
            [w / total for w in weights] + [jnp.zeros((120, 128), F32)], axis=0
        )
        shares = jnp.transpose(shares)[:SPAN]
        mine = o_out[f, h].astype(F32) * shares[:, 0:1]
        for d in range(1, 8):
            mine += o_in[d, h].astype(F32) * shares[:, d : d + 1]
        att[f, h] = mine.astype(BF16)
    def pass_on(ref, device):
        return links.start(ref, ref, device)

    core_waits = [pass_on(att.at[f], me.core())]
    x_waits = [
        (pass_on(att.at[f], me.at_x((x + d) % 4)), (x + 4 - d) % 4) for d in (2, 1, 3)
    ]

    load_wo.wait()
    load_r.wait()
    load_g.wait()
    load_u.wait()
    rw[...] = jnp.zeros((128, WIDTH), BF16)
    rw[0:REST] = gw[MAIN:HID]
    rw[64 : 64 + REST] = uw[MAIN:HID]
    for copy, source in (x_waits[1], x_waits[2], x_waits[0]):
        arrived(copy)
        core_waits.append(pass_on(att.at[source * 2 + c], me.core()))
    arrived(*core_waits)
    attn = jnp.concatenate([att[q, h] for h in range(2) for q in range(8)], axis=1)
    part = jnp.dot(attn, wo[...], preferred_element_type=F32)
    for j in range(4):
        piece = part[:, j * 256 : (j + 1) * 256]
        part_f[j] = piece
        part_b[j] = piece.astype(BF16)
    waits = []
    for d in range(1, 4):
        to = (t + d) % 4
        waits.append(links.start(part_b.at[to], part_in.at[d - 1], me.tp(to)))
    arrived(*waits)
    h1 = part_f[t] + resid_ref[:, pl.ds(pl.multiple_of(t * 256, 256), 256)].astype(F32)
    for d in range(3):
        h1 += part_in[d].astype(F32)
    h1 = h1.astype(BF16)
    h_ref[z, y] = h1

    low, high = pl.ds(0, 48), pl.ds(48, 48)

    gain = gain_ref[...].astype(F32).reshape(1, WIDTH)
    lane = lax.broadcasted_iota(jnp.int32, (SPAN, 128), 1)
    squares = [jnp.zeros((SPAN, 128), F32)]

    def rows_of(side, row):
        return jnp.concatenate(
            [h_ref[side * 4 + k, row] for k in range(4)], axis=1
        ).astype(F32)

    def prepare(row):
        for side in range(2):
            rows = rows_of(side, row)
            squares[0] = jnp.where(
                lane == row * 2 + side, jnp.sum(rows * rows, axis=1, keepdims=True), squares[0]
            )
            xs[side, row] = (rows * gain).astype(BF16)

    def along_z(row, seen):
        mine = h_ref.at[z, row]
        right2, left2 = pass_on(mine, me.at_z(2)), pass_on(mine, me.at_z(-2))
        right1, left1 = pass_on(mine, me.at_z(1)), pass_on(mine, me.at_z(-1))
        seen(z)
        yield
        at = (z + 6) % 8
        arrived(right2)
        right3 = pass_on(h_ref.at[at, row], me.at_z(1))
        right4 = pass_on(h_ref.at[at, row, low], me.at_z(2))
        far = (z + 2) % 8
        arrived(left2)
        left3 = pass_on(h_ref.at[far, row], me.at_z(-1))
        left4 = pass_on(h_ref.at[far, row, high], me.at_z(-2))
        arrived(right1)
        seen((z + 7) % 8)
        arrived(left1)
        seen((z + 1) % 8)
        seen(at)
        seen(far)
        yield
        arrived(right4, left4)
        seen((z + 4) % 8)
        arrived(right3)
        seen((z + 5) % 8)
        arrived(left3)
        seen((z + 3) % 8)

    def own_rows():
        waits = {1: [], 3: []}

        def seen(at):
            for d in (1, 3):
                waits[d].append(pass_on(h_ref.at[at, y], me.at_y_step(d)))

        yield from along_z(y, seen)
        prepare(y)
        yield
        arrived(*waits[1])
        prepare((y + 3) % 4)
        arrived(*waits[3])
        prepare((y + 1) % 4)

    def opposite_rows():
        copy = pass_on(h_ref.at[z, y], me.at_y_step(2))
        yield
        arrived(copy)
        yield from along_z((y + 2) % 4, lambda at: None)
        prepare((y + 2) % 4)

    in_turn(opposite_rows(), own_rows())

    chunks = (pl.ds(0, 1024), pl.ds(1024, MAIN))

    def project(side, dst, k):
        rows = xs[side].reshape(4 * SPAN, WIDTH)
        parts = ((gw, 0, MAIN), (rw, MAIN, 128)) if k == 0 else ((uw, 1024, MAIN),)
        for w, base, size in parts:
            out = lax.dot_general(rows, w[0:size], NT, preferred_element_type=F32)
            dst[:, :, :, base : base + size] = out.astype(dst.dtype).reshape(4, 2, 48, size)

    def to_core(k):
        project(1 - c, send_core, k)
        at = (slice(None), slice(None), slice(None), chunks[k])
        return links.start(send_core.at[at], recv_core.at[at], me.core())

    def joined(i, half, cols):
        return keep[i, half, :, cols] + recv_core[i, half, :, cols].astype(F32)

    def push(k, half, slot, i, device):
        cols = chunks[k]
        stage[i, half, :, cols] = joined(i, half, cols).astype(BF16)
        return links.start(
            stage.at[i, half, :, cols], recv_one.at[half, slot, :, cols], device
        )

    def first_step(k):
        return (
            push(k, 0, 1, 3 - me.xa, me.at_x(me.xa)),
            push(k, 1, 1, flip(me.xb), me.at_x(me.xb)),
            push(k, 0, 0, me.xa, me.at_x(me.xa)),
            push(k, 1, 0, me.xb, me.at_x(me.xb)),
        )

    def second_step(k, far, half, i, device):
        cols = chunks[k]
        arrived(far)
        stage[i, half, :, cols] = plus(
            joined(i, half, cols), recv_one[half, 1, :, cols]
        ).astype(BF16)
        return links.start(stage.at[i, half, :, cols], recv_two.at[half, :, cols], device)

    core_0 = to_core(0)
    project(c, keep, 0)
    core_1 = to_core(1)
    arrived(core_0)
    step_0 = first_step(0)
    project(c, keep, 1)
    arrived(core_1)
    step_1 = first_step(1)
    turned = jnp.transpose(jnp.concatenate([squares[0], jnp.zeros((32, 128), F32)], axis=0))
    for g in range(8):
        sq_out[g] = jnp.broadcast_to(turned[g : g + 1], (8, 128))
    sq_waits = []
    for d in range(1, 8):
        to = (f + d) % 8
        sq_waits.append(links.start(sq_out.at[to], sq_in.at[d - 1], me.ffn(to)))
    own_h[...] = rows_of(me.zh, y)
    two_a, two_b = [], []
    for k, step in ((0, step_0), (1, step_1)):
        two_a.append(second_step(k, step[0], 0, me.xb, me.at_x(me.xb)))
        two_b.append(second_step(k, step[1], 1, me.xa, me.at_x(me.xa)))

    arrived(*sq_waits)
    total = sq_out[f]
    for d in range(7):
        total += sq_in[d]
    total = jnp.transpose(jnp.concatenate([total] * 16, axis=0))
    rs = lax.rsqrt(total / D + 1e-06)[:SPAN, 0:1]

    def silu(v):
        return v / (1.0 + jnp.exp(-v))

    def activate(half):
        both = plus(joined(x, half, slice(None)), recv_one[half, 0], recv_two[half])
        both = both * rs[half * 48 : (half + 1) * 48]
        rest = both[:, MAIN:1024]
        hid[c, x, half, :, 0:MAIN] = (silu(both[:, :MAIN]) * both[:, 1024:]).astype(BF16)
        hid[c, x, half, :, MAIN:] = (silu(rest) * pltpu.roll(rest, 64, 1)).astype(BF16)

    def share(half, i, device):
        return pass_on(hid.at[c, i, half], device)

    arrived(step_0[2], step_1[2], *two_a)
    activate(0)
    a0 = share(0, x, me.at_x(me.xa))
    b0 = share(0, x, me.at_x(me.xb))
    core_waits = [share(0, x, me.core())]
    arrived(step_0[3], step_1[3], *two_b)
    activate(1)
    b1 = share(1, x, me.at_x(me.xb))
    a1 = share(1, x, me.at_x(me.xa))
    core_waits.append(share(1, x, me.core()))
    arrived(a0)
    far_0 = share(0, me.xa, me.at_x(me.xb))
    core_waits.append(share(0, me.xa, me.core()))
    arrived(b1)
    far_1 = share(1, me.xb, me.at_x(me.xa))
    core_waits.append(share(1, me.xb, me.core()))
    arrived(b0)
    core_waits.append(share(0, me.xb, me.core()))
    arrived(a1)
    core_waits.append(share(1, me.xa, me.core()))
    load_d.wait()
    arrived(far_0)
    core_waits.append(share(0, flip(me.xb), me.core()))
    arrived(far_1)
    core_waits.append(share(1, flip(me.xb), me.core()))

    def lower(side):
        rows = hid[side].reshape(4 * SPAN, WIDTH)[:, :HID]
        out = jnp.dot(rows, dw[...], preferred_element_type=F32)
        for i in range(4):
            for k in range(4):
                base = i * SPAN + k * ROWS_OUT
                piece = out[base : base + ROWS_OUT].astype(BF16)
                for j in range(2):
                    pieces[side * 4 + k, i, j] = piece[:, j * 512 : (j + 1) * 512]

    lower(c)
    arrived(*core_waits)
    lower(1 - c)

    def along_z_sum(src, near, relay, half, far):
        copies = []
        for way, sign in ((0, 1), (1, -1)):
            copies.append(
                (
                    links.start(src(3 * sign), relay.at[way], me.at_z(sign)),
                    links.start(src(4).at[way], half.at[way], me.at_z(2 * sign)),
                )
            )
        close = [
            links.start(src(sign), near.at[way], me.at_z(sign))
            for way, sign in ((0, 1), (1, -1))
        ]
        yield
        ends = []
        for way, sign in ((0, 1), (1, -1)):
            ref = src(2 * sign)
            arrived(*copies[way])
            ref[1 - way] = plus(ref[1 - way], relay[way, 1 - way]).astype(BF16)
            ref[way] = plus(ref[way], relay[way, way], half[way]).astype(BF16)
            ends.append(links.start(ref, far.at[way], me.at_z(2 * sign)))
        yield
        src(0)
        arrived(*close, *ends)

    def own_sum():
        waits = {}
        for s in (3, 5, 4, 1, 7, 2, 6, 0):
            at = (z + s) % 8
            waits[s] = [
                links.start(
                    pieces.at[at, (y + d) % 4], from_y.at[d // 2, at], me.at_y_step(d)
                )
                for d in (1, 3)
            ]
        yield

        def src(step):
            at = (z + step + 8) % 8
            if step % 8 in waits:
                arrived(*waits.pop(step % 8))
                summed[at] = plus(pieces[at, y], from_y[0, at], from_y[1, at]).astype(BF16)
            return summed.at[at]

        yield from along_z_sum(src, near.at[0], relay.at[0], halves.at[0], far.at[0])

    def opposite_sum():
        row = (y + 2) % 4
        yield from along_z_sum(
            lambda step: pieces.at[(z + step + 8) % 8, row],
            near.at[1], relay.at[1], halves.at[1], far.at[1],
        )
        done[...] = plus(
            pieces[z, row], near[1, 0], near[1, 1], far[1, 0], far[1, 1]
        ).astype(BF16)
        copy = links.start(done, last, me.at_y_step(2))
        yield
        arrived(copy)

    in_turn(opposite_sum(), own_sum())
    total = plus(summed[z], near[0, 0], near[0, 1], far[0, 0], far[0, 1], last[...])
    down = jnp.concatenate([total[0], total[1]], axis=1)
    start = pl.multiple_of(t * ROWS_OUT, 8)
    out = own_h[pl.ds(start, ROWS_OUT), :] + down
    live = start + lax.broadcasted_iota(jnp.int32, (ROWS_OUT, WIDTH), 0) < length
    out_ref[...] = jnp.where(live, out, 0.0).astype(BF16)
    links.finish()


def layer_call(*args):
    vmem = pl.BlockSpec(memory_space=pltpu.VMEM)
    smem = pl.BlockSpec(memory_space=pltpu.SMEM)
    hbm = pl.BlockSpec(memory_space=pl.ANY)
    copies = 14 + 7 + 3 + 33 + 2 + 7 + 12 + 14 + 33
    piece = (2, ROWS_OUT, 512)
    block = (4, 2, 48, BOTH)
    return pl.pallas_call(
        layer_kernel,
        out_shape=jax.ShapeDtypeStruct((ROWS_OUT, WIDTH), BF16),
        in_specs=[smem, smem, vmem] + [hbm] * 8,
        out_specs=vmem,
        scratch_shapes=[
            pltpu.VMEM((SPAN, 2048), BF16),
            pltpu.VMEM((2, SPAN, 256), BF16),
            pltpu.VMEM((SPAN, WIDTH), BF16),
            pltpu.VMEM((2, KEYS, 256), BF16),
            pltpu.VMEM((2048, WIDTH), BF16),
            pltpu.VMEM((HID, WIDTH), BF16),
            pltpu.VMEM((HID, WIDTH), BF16),
            pltpu.VMEM((128, WIDTH), BF16),
            pltpu.VMEM((HID, WIDTH), BF16),
            pltpu.VMEM((8, 2, SPAN, DH), BF16),
            pltpu.VMEM((8, 2, 8, 128), F32),
            pltpu.VMEM((8, 2, SPAN, DH), BF16),
            pltpu.VMEM((8, 2, 8, 128), F32),
            pltpu.VMEM((8, 2, SPAN, DH), BF16),
            pltpu.VMEM((4, SPAN, 256), F32),
            pltpu.VMEM((4, SPAN, 256), BF16),
            pltpu.VMEM((3, SPAN, 256), BF16),
            pltpu.VMEM((8, 4, SPAN, 256), BF16),
            pltpu.VMEM((2, 4, SPAN, WIDTH), BF16),
            pltpu.VMEM((SPAN, WIDTH), F32),
            pltpu.VMEM((8, 8, 128), F32),
            pltpu.VMEM((7, 8, 128), F32),
            pltpu.VMEM(block, BF16),
            pltpu.VMEM(block, BF16),
            pltpu.VMEM(block, F32),
            pltpu.VMEM(block, BF16),
            pltpu.VMEM((2, 2, 48, BOTH), BF16),
            pltpu.VMEM((2, 48, BOTH), BF16),
            pltpu.VMEM((2, 4, 2, 48, WIDTH), BF16),
            pltpu.VMEM((8, 4) + piece, BF16),
            pltpu.VMEM((2, 8) + piece, BF16),
            pltpu.VMEM((8,) + piece, BF16),
            pltpu.VMEM((2, 2) + piece, BF16),
            pltpu.VMEM((2, 2) + piece, BF16),
            pltpu.VMEM((2, 2, ROWS_OUT, 512), BF16),
            pltpu.VMEM((2, 2) + piece, BF16),
            pltpu.VMEM(piece, BF16),
            pltpu.VMEM(piece, BF16),
            pltpu.SemaphoreType.DMA((9,)),
            pltpu.SemaphoreType.DMA((copies,)),
            pltpu.SemaphoreType.DMA((copies,)),
        ],
        compiler_params=pltpu.CompilerParams(
            collective_id=0, has_side_effects=True, vmem_limit_bytes=60 << 20
        ),
        name="layer",
    )(*args)


def body(
    queries,
    new_kv,
    kv_cache,
    lengths,
    prefixes,
    resid,
    out_weight,
    gain,
    gate_weight,
    up_weight,
    down_weight,
):
    return layer_call(
        lengths,
        prefixes,
        gain,
        queries,
        new_kv,
        resid,
        kv_cache,
        out_weight,
        gate_weight.T,
        up_weight.T,
        down_weight,
    )


def solution(mesh):
    return jax.shard_map(
        body,
        mesh=mesh,
        in_specs=(
            P("grp", "tp"),
            P(None, "grp", "tp"),
            P(None, "grp", "ffn", "tp"),
            P("grp"),
            P("grp"),
            P("grp", "ffn"),
            P("tp", "ffn"),
            P("ffn"),
            P("ffn", ("grp", "tp")),
            P("ffn", ("grp", "tp")),
            P(("grp", "tp"), "ffn"),
        ),
        out_specs=P(("grp", "tp"), "ffn"),
        check_vma=False,
    )
```

```python
import functools
import math

import jax
import jax.numpy as jnp
from jax import lax
from jax.experimental import pallas as pl
from jax.experimental.pallas import tpu as pltpu
from jax.sharding import PartitionSpec as P

MESH = pl.DeviceIdType.MESH
F32 = jnp.float32
BF16 = jnp.bfloat16

D = 8192
DH = 128
SPAN = 96
ROWS_OUT = 24
QUERIES = 2
MAIN = 896
REST = 28
BOTH = 1920
KEYS = 2048
WIDTH = 1024
HID = 924
NEG = -1e30
SCALE = math.log2(math.e) / math.sqrt(DH)


class Place:
    def __init__(self):
        g = lax.axis_index("grp")
        self.t = lax.axis_index("tp")
        self.f = lax.axis_index("ffn")
        self.y, self.zh = g // 2, g % 2
        self.x, self.c = self.f // 2, self.f % 2
        self.z = self.zh * 4 + self.t
        self.xa, self.xb = flip(self.x), 3 - self.x
        self.ya, self.yb = flip(self.y), 3 - self.y

    def ffn(self, f):
        return {"ffn": f}

    def tp(self, t):
        return {"tp": t}

    def core(self):
        return {"ffn": self.x * 2 + 1 - self.c}

    def at_x(self, x):
        return {"ffn": x * 2 + self.c}

    def at_y(self, y):
        return {"grp": y * 2 + self.zh}

    def at_y_step(self, step):
        return self.at_y((self.y + step) % 4)

    def at_z(self, step):
        z = (self.z + step + 8) % 8
        return {"grp": self.y * 2 + z // 4, "tp": z % 4}


def flip(v):
    return v + 1 - 2 * (v % 2)


class Links:
    def __init__(self, send_sems, recv_sems):
        self.send_sems, self.recv_sems = send_sems, recv_sems
        self.started = []

    def start(self, src, dst, device):
        copy = self.make(src, dst, device)
        copy.start()
        return copy

    def make(self, src, dst, device):
        k = len(self.started)
        copy = pltpu.make_async_remote_copy(
            src_ref=src,
            dst_ref=dst,
            send_sem=self.send_sems.at[k],
            recv_sem=self.recv_sems.at[k],
            device_id=device,
            device_id_type=MESH,
        )
        self.started.append(copy)
        return copy

    def finish(self):
        for copy in self.started:
            copy.wait_send()


def greet(devices):
    barrier = pltpu.get_barrier_semaphore()
    for device in devices:
        pl.semaphore_signal(barrier, inc=1, device_id=device, device_id_type=MESH)


def greeted(devices):
    pl.semaphore_wait(pltpu.get_barrier_semaphore(), len(devices))


def in_turn(*flows):
    alive = list(flows)
    while alive:
        for flow in list(alive):
            try:
                next(flow)
            except StopIteration:
                alive.remove(flow)


def arrived(*copies):
    for copy in copies:
        copy.wait_recv()


NT = (((1,), (1,)), ((), ()))


def plus(*parts):
    out = parts[0].astype(F32)
    for part in parts[1:]:
        out += part.astype(F32)
    return out


def layer_kernel(
    length_ref, prefix_ref, gain_ref,
    q_hbm, new_hbm, resid_hbm, cache_hbm, wo_hbm, gate_hbm, up_hbm, down_hbm,
    out_ref,
    q_ref, new_ref, resid_ref, kv, wo, gw, uw, rw, dw,
    o_out, st_out, o_in, st_in, att, part_f, part_b, part_in, h_ref,
    xs, own_h, sq_out, sq_in,
    send_core, recv_core, keep, stage, recv_one, recv_two, hid,
    pieces, from_y, summed, near, relay, halves, far, done, last,
    local_sems, send_sems, recv_sems,
):
    me = Place()
    links = Links(send_sems, recv_sems)
    f, t, y, z, x, c = me.f, me.t, me.y, me.z, me.x, me.c

    def load(k, src, dst):
        copy = pltpu.make_async_copy(src, dst, local_sems.at[k])
        copy.start()
        return copy

    first = [
        load(0, q_hbm, q_ref),
        load(1, cache_hbm.at[0, 0], kv.at[0]),
        load(2, new_hbm, new_ref),
        load(3, cache_hbm.at[1, 0], kv.at[1]),
    ]
    friends = [me.ffn((f + d) % 8) for d in range(1, 8)]
    friends += [me.tp((t + d) % 4) for d in range(1, 4)]
    friends += [me.at_y_step(d) for d in range(1, 4)]
    friends += [me.at_z(step) for step in (1, -1, 2, -2)]
    greet(friends)

    length, prefix = length_ref[0], prefix_ref[0]
    lanes = lax.broadcasted_iota(jnp.int32, (1, KEYS), 1)
    bias = jnp.where(f * KEYS + lanes < prefix, 0.0, NEG).astype(F32)
    slot = lax.broadcasted_iota(jnp.int32, (SPAN, SPAN), 0)
    key = lax.broadcasted_iota(jnp.int32, (SPAN, SPAN), 1)
    limit = jnp.where(f == 0, length, 0)
    new_bias = jnp.where((key <= slot) & (key < limit), 0.0, NEG).astype(F32)
    new_bias = jnp.concatenate([new_bias] * QUERIES, axis=0)
    lane = lax.broadcasted_iota(jnp.int32, (QUERIES * SPAN, 128), 1)
    for copy in first:
        copy.wait()
    load_wo = load(4, wo_hbm, wo)
    load_r = load(5, resid_hbm, resid_ref)
    load_g = load(6, gate_hbm, gw)
    load_u = load(7, up_hbm, uw)
    load_d = load(8, down_hbm, dw)

    def attend(half, h):
        cols = pl.ds(pl.multiple_of(h * DH, DH), DH)
        keys, values = kv[0, :, cols], kv[1, :, cols]
        new_keys, new_values = new_ref[0, :, cols], new_ref[1, :, cols]
        wide = jnp.concatenate([values, jnp.ones((KEYS, DH), BF16)], axis=1)
        wide_new = jnp.concatenate([new_values, jnp.ones((SPAN, DH), BF16)], axis=1)
        for first_q in range(half * 4, half * 4 + 4, QUERIES):
            q = jnp.concatenate(
                [
                    q_ref[:, pl.ds(pl.multiple_of((h * 8 + first_q + i) * DH, DH), DH)]
                    for i in range(QUERIES)
                ],
                axis=0,
            )
            s = lax.dot_general(q, keys, NT, preferred_element_type=F32) + bias
            s_new = lax.dot_general(q, new_keys, NT, preferred_element_type=F32) + new_bias
            top = jnp.maximum(
                jnp.max(s, axis=1, keepdims=True), jnp.max(s_new, axis=1, keepdims=True)
            )
            p = jnp.exp2((s - top) * SCALE).astype(BF16)
            p_new = jnp.exp2((s_new - top) * SCALE).astype(BF16)
            acc = jnp.dot(p, wide, preferred_element_type=F32) + jnp.dot(
                p_new, wide_new, preferred_element_type=F32
            )
            total = acc[:, DH:]
            out = (acc[:, :DH] / total).astype(BF16)
            stats = jnp.where(lane == 0, top, jnp.where(lane == 1, total, 0.0))
            for i in range(QUERIES):
                rows = slice(i * SPAN, (i + 1) * SPAN)
                o_out[first_q + i, h] = out[rows]
                square = jnp.concatenate([stats[rows], jnp.zeros((32, 128), F32)], axis=0)
                st_out[first_q + i, h] = jnp.transpose(square)[:8]

    exchange = []
    for d in (2, 6, 3, 5, 4, 7, 1):
        to = (f + d) % 8
        exchange.append((to, links.make(st_out.at[to], st_in.at[d], me.ffn(to))))
        exchange.append((to, links.make(o_out.at[to], o_in.at[d], me.ffn(to))))
    for half in range(2):

        for h in range(2):
            attend(half, h)

        if half == 0:
            greeted(friends)
        for to, copy in exchange:
            pl.when(to // 4 == half)(copy.start)
    arrived(*[copy for to, copy in exchange])
    for h in range(2):
        stats = [st_out[f, h]] + [st_in[d, h] for d in range(1, 8)]
        tops = [s[0:1] for s in stats]
        top = functools.reduce(jnp.maximum, tops)
        weights = [s[1:2] * jnp.exp2((m - top) * SCALE) for s, m in zip(stats, tops)]
        total = sum(weights[1:], weights[0])
        shares = jnp.concatenate(
            [w / total for w in weights] + [jnp.zeros((120, 128), F32)], axis=0
        )
        shares = jnp.transpose(shares)[:SPAN]
        mine = o_out[f, h].astype(F32) * shares[:, 0:1]
        for d in range(1, 8):
            mine += o_in[d, h].astype(F32) * shares[:, d : d + 1]
        att[f, h] = mine.astype(BF16)
    def pass_on(ref, device):
        return links.start(ref, ref, device)

    core_waits = [pass_on(att.at[f], me.core())]
    x_waits = [
        (pass_on(att.at[f], me.at_x((x + d) % 4)), (x + 4 - d) % 4) for d in (2, 1, 3)
    ]

    load_wo.wait()
    load_r.wait()
    load_g.wait()
    load_u.wait()
    rw[...] = jnp.zeros((128, WIDTH), BF16)
    rw[0:REST] = gw[MAIN:HID]
    rw[64 : 64 + REST] = uw[MAIN:HID]
    for copy, source in (x_waits[1], x_waits[2], x_waits[0]):
        arrived(copy)
        core_waits.append(pass_on(att.at[source * 2 + c], me.core()))
    arrived(*core_waits)
    attn = jnp.concatenate([att[q, h] for h in range(2) for q in range(8)], axis=1)
    part = jnp.dot(attn, wo[...], preferred_element_type=F32)
    for j in range(4):
        piece = part[:, j * 256 : (j + 1) * 256]
        part_f[j] = piece
        part_b[j] = piece.astype(BF16)
    waits = []
    for d in range(1, 4):
        to = (t + d) % 4
        waits.append(links.start(part_b.at[to], part_in.at[d - 1], me.tp(to)))
    arrived(*waits)
    h1 = part_f[t] + resid_ref[:, pl.ds(pl.multiple_of(t * 256, 256), 256)].astype(F32)
    for d in range(3):
        h1 += part_in[d].astype(F32)
    h1 = h1.astype(BF16)
    h_ref[z, y] = h1

    low, high = pl.ds(0, 48), pl.ds(48, 48)

    gain = gain_ref[...].astype(F32).reshape(1, WIDTH)
    lane = lax.broadcasted_iota(jnp.int32, (SPAN, 128), 1)
    squares = [jnp.zeros((SPAN, 128), F32)]

    def rows_of(side, row):
        return jnp.concatenate(
            [h_ref[side * 4 + k, row] for k in range(4)], axis=1
        ).astype(F32)

    def prepare(row):
        for side in range(2):
            rows = rows_of(side, row)
            squares[0] = jnp.where(
                lane == row * 2 + side, jnp.sum(rows * rows, axis=1, keepdims=True), squares[0]
            )
            xs[side, row] = (rows * gain).astype(BF16)

    def along_z(row, seen):
        mine = h_ref.at[z, row]
        right2, left2 = pass_on(mine, me.at_z(2)), pass_on(mine, me.at_z(-2))
        right1, left1 = pass_on(mine, me.at_z(1)), pass_on(mine, me.at_z(-1))
        seen(z)
        yield
        at = (z + 6) % 8
        arrived(right2)
        right3 = pass_on(h_ref.at[at, row], me.at_z(1))
        right4 = pass_on(h_ref.at[at, row, low], me.at_z(2))
        far = (z + 2) % 8
        arrived(left2)
        left3 = pass_on(h_ref.at[far, row], me.at_z(-1))
        left4 = pass_on(h_ref.at[far, row, high], me.at_z(-2))
        arrived(right1)
        seen((z + 7) % 8)
        arrived(left1)
        seen((z + 1) % 8)
        seen(at)
        seen(far)
        yield
        arrived(right4, left4)
        seen((z + 4) % 8)
        arrived(right3)
        seen((z + 5) % 8)
        arrived(left3)
        seen((z + 3) % 8)

    def own_rows():
        waits = {1: [], 3: []}

        def seen(at):
            for d in (1, 3):
                waits[d].append(pass_on(h_ref.at[at, y], me.at_y_step(d)))

        yield from along_z(y, seen)
        prepare(y)
        yield
        arrived(*waits[1])
        prepare((y + 3) % 4)
        arrived(*waits[3])
        prepare((y + 1) % 4)

    def opposite_rows():
        copy = pass_on(h_ref.at[z, y], me.at_y_step(2))
        yield
        arrived(copy)
        yield from along_z((y + 2) % 4, lambda at: None)
        prepare((y + 2) % 4)

    in_turn(opposite_rows(), own_rows())

    chunks = (pl.ds(0, 1024), pl.ds(1024, MAIN))

    def project(side, dst, k):
        rows = xs[side].reshape(4 * SPAN, WIDTH)
        parts = ((gw, 0, MAIN), (rw, MAIN, 128)) if k == 0 else ((uw, 1024, MAIN),)
        for w, base, size in parts:
            out = lax.dot_general(rows, w[0:size], NT, preferred_element_type=F32)
            dst[:, :, :, base : base + size] = out.astype(dst.dtype).reshape(4, 2, 48, size)

    def to_core(k):
        project(1 - c, send_core, k)
        at = (slice(None), slice(None), slice(None), chunks[k])
        return links.start(send_core.at[at], recv_core.at[at], me.core())

    def joined(i, half, cols):
        return keep[i, half, :, cols] + recv_core[i, half, :, cols].astype(F32)

    def push(k, half, slot, i, device):
        cols = chunks[k]
        stage[i, half, :, cols] = joined(i, half, cols).astype(BF16)
        return links.start(
            stage.at[i, half, :, cols], recv_one.at[half, slot, :, cols], device
        )

    def first_step(k):
        return (
            push(k, 0, 1, 3 - me.xa, me.at_x(me.xa)),
            push(k, 1, 1, flip(me.xb), me.at_x(me.xb)),
            push(k, 0, 0, me.xa, me.at_x(me.xa)),
            push(k, 1, 0, me.xb, me.at_x(me.xb)),
        )

    def second_step(k, far, half, i, device):
        cols = chunks[k]
        arrived(far)
        stage[i, half, :, cols] = plus(
            joined(i, half, cols), recv_one[half, 1, :, cols]
        ).astype(BF16)
        return links.start(stage.at[i, half, :, cols], recv_two.at[half, :, cols], device)

    core_0 = to_core(0)
    project(c, keep, 0)
    core_1 = to_core(1)
    arrived(core_0)
    step_0 = first_step(0)
    project(c, keep, 1)
    arrived(core_1)
    step_1 = first_step(1)
    turned = jnp.transpose(jnp.concatenate([squares[0], jnp.zeros((32, 128), F32)], axis=0))
    for g in range(8):
        sq_out[g] = jnp.broadcast_to(turned[g : g + 1], (8, 128))
    sq_waits = []
    for d in range(1, 8):
        to = (f + d) % 8
        sq_waits.append(links.start(sq_out.at[to], sq_in.at[d - 1], me.ffn(to)))
    own_h[...] = rows_of(me.zh, y)
    two_a, two_b = [], []
    for k, step in ((0, step_0), (1, step_1)):
        two_a.append(second_step(k, step[0], 0, me.xb, me.at_x(me.xb)))
        two_b.append(second_step(k, step[1], 1, me.xa, me.at_x(me.xa)))

    arrived(*sq_waits)
    total = sq_out[f]
    for d in range(7):
        total += sq_in[d]
    total = jnp.transpose(jnp.concatenate([total] * 16, axis=0))
    rs = lax.rsqrt(total / D + 1e-06)[:SPAN, 0:1]

    def silu(v):
        return v / (1.0 + jnp.exp(-v))

    def activate(half):
        both = plus(joined(x, half, slice(None)), recv_one[half, 0], recv_two[half])
        both = both * rs[half * 48 : (half + 1) * 48]
        rest = both[:, MAIN:1024]
        hid[c, x, half, :, 0:MAIN] = (silu(both[:, :MAIN]) * both[:, 1024:]).astype(BF16)
        hid[c, x, half, :, MAIN:] = (silu(rest) * pltpu.roll(rest, 64, 1)).astype(BF16)

    def share(half, i, device):
        return pass_on(hid.at[c, i, half], device)

    arrived(step_0[2], step_1[2], *two_a)
    activate(0)
    a0 = share(0, x, me.at_x(me.xa))
    b0 = share(0, x, me.at_x(me.xb))
    core_waits = [share(0, x, me.core())]
    arrived(step_0[3], step_1[3], *two_b)
    activate(1)
    b1 = share(1, x, me.at_x(me.xb))
    a1 = share(1, x, me.at_x(me.xa))
    core_waits.append(share(1, x, me.core()))
    arrived(a0)
    far_0 = share(0, me.xa, me.at_x(me.xb))
    core_waits.append(share(0, me.xa, me.core()))
    arrived(b1)
    far_1 = share(1, me.xb, me.at_x(me.xa))
    core_waits.append(share(1, me.xb, me.core()))
    arrived(b0)
    core_waits.append(share(0, me.xb, me.core()))
    arrived(a1)
    core_waits.append(share(1, me.xa, me.core()))
    load_d.wait()
    arrived(far_0)
    core_waits.append(share(0, flip(me.xb), me.core()))
    arrived(far_1)
    core_waits.append(share(1, flip(me.xb), me.core()))

    def lower(side):
        rows = hid[side].reshape(4 * SPAN, WIDTH)[:, :HID]
        out = jnp.dot(rows, dw[...], preferred_element_type=F32)
        for i in range(4):
            for k in range(4):
                base = i * SPAN + k * ROWS_OUT
                piece = out[base : base + ROWS_OUT].astype(BF16)
                for j in range(2):
                    pieces[side * 4 + k, i, j] = piece[:, j * 512 : (j + 1) * 512]

    lower(c)
    arrived(*core_waits)
    lower(1 - c)

    def along_z_sum(src, near, relay, half, far):
        copies = []
        for way, sign in ((0, 1), (1, -1)):
            copies.append(
                (
                    links.start(src(3 * sign), relay.at[way], me.at_z(sign)),
                    links.start(src(4).at[way], half.at[way], me.at_z(2 * sign)),
                )
            )
        close = [
            links.start(src(sign), near.at[way], me.at_z(sign))
            for way, sign in ((0, 1), (1, -1))
        ]
        yield
        ends = []
        for way, sign in ((0, 1), (1, -1)):
            ref = src(2 * sign)
            arrived(*copies[way])
            ref[1 - way] = plus(ref[1 - way], relay[way, 1 - way]).astype(BF16)
            ref[way] = plus(ref[way], relay[way, way], half[way]).astype(BF16)
            ends.append(links.start(ref, far.at[way], me.at_z(2 * sign)))
        yield
        src(0)
        arrived(*close, *ends)

    def own_sum():
        waits = {}
        for s in (3, 5, 4, 1, 7, 2, 6, 0):
            at = (z + s) % 8
            waits[s] = [
                links.start(
                    pieces.at[at, (y + d) % 4], from_y.at[d // 2, at], me.at_y_step(d)
                )
                for d in (1, 3)
            ]
        yield

        def src(step):
            at = (z + step + 8) % 8
            if step % 8 in waits:
                arrived(*waits.pop(step % 8))
                summed[at] = plus(pieces[at, y], from_y[0, at], from_y[1, at]).astype(BF16)
            return summed.at[at]

        yield from along_z_sum(src, near.at[0], relay.at[0], halves.at[0], far.at[0])

    def opposite_sum():
        row = (y + 2) % 4
        yield from along_z_sum(
            lambda step: pieces.at[(z + step + 8) % 8, row],
            near.at[1], relay.at[1], halves.at[1], far.at[1],
        )
        done[...] = plus(
            pieces[z, row], near[1, 0], near[1, 1], far[1, 0], far[1, 1]
        ).astype(BF16)
        copy = links.start(done, last, me.at_y_step(2))
        yield
        arrived(copy)

    in_turn(opposite_sum(), own_sum())
    total = plus(summed[z], near[0, 0], near[0, 1], far[0, 0], far[0, 1], last[...])
    down = jnp.concatenate([total[0], total[1]], axis=1)
    start = pl.multiple_of(t * ROWS_OUT, 8)
    out = own_h[pl.ds(start, ROWS_OUT), :] + down
    live = start + lax.broadcasted_iota(jnp.int32, (ROWS_OUT, WIDTH), 0) < length
    out_ref[...] = jnp.where(live, out, 0.0).astype(BF16)
    links.finish()


def layer_call(*args):
    vmem = pl.BlockSpec(memory_space=pltpu.VMEM)
    smem = pl.BlockSpec(memory_space=pltpu.SMEM)
    hbm = pl.BlockSpec(memory_space=pl.ANY)
    copies = 14 + 7 + 3 + 33 + 2 + 7 + 12 + 14 + 33
    piece = (2, ROWS_OUT, 512)
    block = (4, 2, 48, BOTH)
    return pl.pallas_call(
        layer_kernel,
        out_shape=jax.ShapeDtypeStruct((ROWS_OUT, WIDTH), BF16),
        in_specs=[smem, smem, vmem] + [hbm] * 8,
        out_specs=vmem,
        scratch_shapes=[
            pltpu.VMEM((SPAN, 2048), BF16),
            pltpu.VMEM((2, SPAN, 256), BF16),
            pltpu.VMEM((SPAN, WIDTH), BF16),
            pltpu.VMEM((2, KEYS, 256), BF16),
            pltpu.VMEM((2048, WIDTH), BF16),
            pltpu.VMEM((HID, WIDTH), BF16),
            pltpu.VMEM((HID, WIDTH), BF16),
            pltpu.VMEM((128, WIDTH), BF16),
            pltpu.VMEM((HID, WIDTH), BF16),
            pltpu.VMEM((8, 2, SPAN, DH), BF16),
            pltpu.VMEM((8, 2, 8, 128), F32),
            pltpu.VMEM((8, 2, SPAN, DH), BF16),
            pltpu.VMEM((8, 2, 8, 128), F32),
            pltpu.VMEM((8, 2, SPAN, DH), BF16),
            pltpu.VMEM((4, SPAN, 256), F32),
            pltpu.VMEM((4, SPAN, 256), BF16),
            pltpu.VMEM((3, SPAN, 256), BF16),
            pltpu.VMEM((8, 4, SPAN, 256), BF16),
            pltpu.VMEM((2, 4, SPAN, WIDTH), BF16),
            pltpu.VMEM((SPAN, WIDTH), F32),
            pltpu.VMEM((8, 8, 128), F32),
            pltpu.VMEM((7, 8, 128), F32),
            pltpu.VMEM(block, BF16),
            pltpu.VMEM(block, BF16),
            pltpu.VMEM(block, F32),
            pltpu.VMEM(block, BF16),
            pltpu.VMEM((2, 2, 48, BOTH), BF16),
            pltpu.VMEM((2, 48, BOTH), BF16),
            pltpu.VMEM((2, 4, 2, 48, WIDTH), BF16),
            pltpu.VMEM((8, 4) + piece, BF16),
            pltpu.VMEM((2, 8) + piece, BF16),
            pltpu.VMEM((8,) + piece, BF16),
            pltpu.VMEM((2, 2) + piece, BF16),
            pltpu.VMEM((2, 2) + piece, BF16),
            pltpu.VMEM((2, 2, ROWS_OUT, 512), BF16),
            pltpu.VMEM((2, 2) + piece, BF16),
            pltpu.VMEM(piece, BF16),
            pltpu.VMEM(piece, BF16),
            pltpu.SemaphoreType.DMA((9,)),
            pltpu.SemaphoreType.DMA((copies,)),
            pltpu.SemaphoreType.DMA((copies,)),
        ],
        compiler_params=pltpu.CompilerParams(
            collective_id=0, has_side_effects=True, vmem_limit_bytes=60 << 20
        ),
        name="layer",
    )(*args)


def body(
    queries,
    new_kv,
    kv_cache,
    lengths,
    prefixes,
    resid,
    out_weight,
    gain,
    gate_weight,
    up_weight,
    down_weight,
):
    return layer_call(
        lengths,
        prefixes,
        gain,
        queries,
        new_kv,
        resid,
        kv_cache,
        out_weight,
        gate_weight.T,
        up_weight.T,
        down_weight,
    )


def solution(mesh):
    return jax.shard_map(
        body,
        mesh=mesh,
        in_specs=(
            P("grp", "tp"),
            P(None, "grp", "tp"),
            P(None, "grp", "ffn", "tp"),
            P("grp"),
            P("grp"),
            P("grp", "ffn"),
            P("tp", "ffn"),
            P("ffn"),
            P("ffn", ("grp", "tp")),
            P("ffn", ("grp", "tp")),
            P(("grp", "tp"), "ffn"),
        ),
        out_specs=P(("grp", "tp"), "ffn"),
        check_vma=False,
    )
```

```python
import functools
import math

import jax
import jax.numpy as jnp
from jax import lax
from jax.experimental import pallas as pl
from jax.experimental.pallas import tpu as pltpu
from jax.sharding import PartitionSpec as P

MESH = pl.DeviceIdType.MESH
F32 = jnp.float32
BF16 = jnp.bfloat16

D = 8192
DH = 128
SPAN = 96
ROWS_OUT = 24
QUERIES = 2
MAIN = 896
REST = 28
BOTH = 1920
KEYS = 2048
WIDTH = 1024
HID = 924
NEG = -1e30
SCALE = math.log2(math.e) / math.sqrt(DH)


class Place:
    def __init__(self):
        g = lax.axis_index("grp")
        self.t = lax.axis_index("tp")
        self.f = lax.axis_index("ffn")
        self.y, self.zh = g // 2, g % 2
        self.x, self.c = self.f // 2, self.f % 2
        self.z = self.zh * 4 + self.t
        self.xa, self.xb = flip(self.x), 3 - self.x
        self.ya, self.yb = flip(self.y), 3 - self.y

    def ffn(self, f):
        return {"ffn": f}

    def tp(self, t):
        return {"tp": t}

    def core(self):
        return {"ffn": self.x * 2 + 1 - self.c}

    def at_x(self, x):
        return {"ffn": x * 2 + self.c}

    def at_y(self, y):
        return {"grp": y * 2 + self.zh}

    def at_y_step(self, step):
        return self.at_y((self.y + step) % 4)

    def at_z(self, step):
        z = (self.z + step + 8) % 8
        return {"grp": self.y * 2 + z // 4, "tp": z % 4}


def flip(v):
    return v + 1 - 2 * (v % 2)


class Links:
    def __init__(self, send_sems, recv_sems):
        self.send_sems, self.recv_sems = send_sems, recv_sems
        self.started = []

    def start(self, src, dst, device):
        copy = self.make(src, dst, device)
        copy.start()
        return copy

    def make(self, src, dst, device):
        k = len(self.started)
        copy = pltpu.make_async_remote_copy(
            src_ref=src,
            dst_ref=dst,
            send_sem=self.send_sems.at[k],
            recv_sem=self.recv_sems.at[k],
            device_id=device,
            device_id_type=MESH,
        )
        self.started.append(copy)
        return copy

    def finish(self):
        for copy in self.started:
            copy.wait_send()


def greet(devices):
    barrier = pltpu.get_barrier_semaphore()
    for device in devices:
        pl.semaphore_signal(barrier, inc=1, device_id=device, device_id_type=MESH)


def greeted(devices):
    pl.semaphore_wait(pltpu.get_barrier_semaphore(), len(devices))


def in_turn(*flows):
    alive = list(flows)
    while alive:
        for flow in list(alive):
            try:
                next(flow)
            except StopIteration:
                alive.remove(flow)


def arrived(*copies):
    for copy in copies:
        copy.wait_recv()


NT = (((1,), (1,)), ((), ()))


def plus(*parts):
    out = parts[0].astype(F32)
    for part in parts[1:]:
        out += part.astype(F32)
    return out


def layer_kernel(
    length_ref, prefix_ref, gain_ref,
    q_hbm, new_hbm, resid_hbm, cache_hbm, wo_hbm, gate_hbm, up_hbm, down_hbm,
    out_ref,
    q_ref, new_ref, resid_ref, kv, wo, gw, uw, rw, dw,
    o_out, st_out, o_in, st_in, att, part_f, part_b, part_in, h_ref,
    xs, own_h, sq_out, sq_in,
    send_core, recv_core, keep, stage, recv_one, recv_two, hid,
    pieces, from_y, summed, near, relay, halves, far, done, last,
    local_sems, send_sems, recv_sems,
):
    me = Place()
    links = Links(send_sems, recv_sems)
    f, t, y, z, x, c = me.f, me.t, me.y, me.z, me.x, me.c

    def load(k, src, dst):
        copy = pltpu.make_async_copy(src, dst, local_sems.at[k])
        copy.start()
        return copy

    first = [
        load(0, q_hbm, q_ref),
        load(1, cache_hbm.at[0, 0], kv.at[0]),
        load(2, new_hbm, new_ref),
        load(3, cache_hbm.at[1, 0], kv.at[1]),
    ]
    friends = [me.ffn((f + d) % 8) for d in range(1, 8)]
    friends += [me.tp((t + d) % 4) for d in range(1, 4)]
    friends += [me.at_y_step(d) for d in range(1, 4)]
    friends += [me.at_z(step) for step in (1, -1, 2, -2)]
    greet(friends)

    length, prefix = length_ref[0], prefix_ref[0]
    lanes = lax.broadcasted_iota(jnp.int32, (1, KEYS), 1)
    bias = jnp.where(f * KEYS + lanes < prefix, 0.0, NEG).astype(F32)
    slot = lax.broadcasted_iota(jnp.int32, (SPAN, SPAN), 0)
    key = lax.broadcasted_iota(jnp.int32, (SPAN, SPAN), 1)
    limit = jnp.where(f == 0, length, 0)
    new_bias = jnp.where((key <= slot) & (key < limit), 0.0, NEG).astype(F32)
    new_bias = jnp.concatenate([new_bias] * QUERIES, axis=0)
    lane = lax.broadcasted_iota(jnp.int32, (QUERIES * SPAN, 128), 1)
    for copy in first:
        copy.wait()
    load_wo = load(4, wo_hbm, wo)
    load_r = load(5, resid_hbm, resid_ref)
    load_g = load(6, gate_hbm, gw)
    load_u = load(7, up_hbm, uw)
    load_d = load(8, down_hbm, dw)

    def attend(phase, h):
        cols = pl.ds(pl.multiple_of(h * DH, DH), DH)
        keys, values = kv[0, :, cols], kv[1, :, cols]
        new_keys, new_values = new_ref[0, :, cols], new_ref[1, :, cols]
        wide = jnp.concatenate([values, jnp.ones((KEYS, DH), BF16)], axis=1)
        wide_new = jnp.concatenate([new_values, jnp.ones((SPAN, DH), BF16)], axis=1)
        for first_q in range(phase[0], phase[1], QUERIES):
            q = jnp.concatenate(
                [
                    q_ref[:, pl.ds(pl.multiple_of((h * 8 + first_q + i) * DH, DH), DH)]
                    for i in range(QUERIES)
                ],
                axis=0,
            )
            s = lax.dot_general(q, keys, NT, preferred_element_type=F32) + bias
            s_new = lax.dot_general(q, new_keys, NT, preferred_element_type=F32) + new_bias
            top = jnp.maximum(
                jnp.max(s, axis=1, keepdims=True), jnp.max(s_new, axis=1, keepdims=True)
            )
            p = jnp.exp2((s - top) * SCALE).astype(BF16)
            p_new = jnp.exp2((s_new - top) * SCALE).astype(BF16)
            acc = jnp.dot(p, wide, preferred_element_type=F32) + jnp.dot(
                p_new, wide_new, preferred_element_type=F32
            )
            total = acc[:, DH:]
            out = (acc[:, :DH] / total).astype(BF16)
            stats = jnp.where(lane == 0, top, jnp.where(lane == 1, total, 0.0))
            for i in range(QUERIES):
                rows = slice(i * SPAN, (i + 1) * SPAN)
                o_out[first_q + i, h] = out[rows]
                square = jnp.concatenate([stats[rows], jnp.zeros((32, 128), F32)], axis=0)
                st_out[first_q + i, h] = jnp.transpose(square)[:8]

    exchange = []
    for d in (2, 6, 3, 5, 4, 7, 1):
        to = (f + d) % 8
        exchange.append((to, links.make(st_out.at[to], st_in.at[d], me.ffn(to))))
        exchange.append((to, links.make(o_out.at[to], o_in.at[d], me.ffn(to))))
    for phase in ((0, 4), (4, 6), (6, 8)):
        for h in range(2):
            attend(phase, h)
        if phase[0] == 0:
            greeted(friends)
        for to, copy in exchange:
            pl.when((to >= phase[0]) & (to < phase[1]))(copy.start)
    arrived(*[copy for to, copy in exchange])
    for h in range(2):
        stats = [st_out[f, h]] + [st_in[d, h] for d in range(1, 8)]
        tops = [s[0:1] for s in stats]
        top = functools.reduce(jnp.maximum, tops)
        weights = [s[1:2] * jnp.exp2((m - top) * SCALE) for s, m in zip(stats, tops)]
        total = sum(weights[1:], weights[0])
        shares = jnp.concatenate(
            [w / total for w in weights] + [jnp.zeros((120, 128), F32)], axis=0
        )
        shares = jnp.transpose(shares)[:SPAN]
        mine = o_out[f, h].astype(F32) * shares[:, 0:1]
        for d in range(1, 8):
            mine += o_in[d, h].astype(F32) * shares[:, d : d + 1]
        att[f, h] = mine.astype(BF16)
    def pass_on(ref, device):
        return links.start(ref, ref, device)

    core_waits = [pass_on(att.at[f], me.core())]
    x_waits = [
        (pass_on(att.at[f], me.at_x((x + d) % 4)), (x + 4 - d) % 4) for d in (2, 1, 3)
    ]

    load_wo.wait()
    load_r.wait()
    load_g.wait()
    load_u.wait()
    rw[...] = jnp.zeros((128, WIDTH), BF16)
    rw[0:REST] = gw[MAIN:HID]
    rw[64 : 64 + REST] = uw[MAIN:HID]
    for copy, source in (x_waits[1], x_waits[2], x_waits[0]):
        arrived(copy)
        core_waits.append(pass_on(att.at[source * 2 + c], me.core()))
    arrived(*core_waits)
    attn = jnp.concatenate([att[q, h] for h in range(2) for q in range(8)], axis=1)
    part = jnp.dot(attn, wo[...], preferred_element_type=F32)
    for j in range(4):
        piece = part[:, j * 256 : (j + 1) * 256]
        part_f[j] = piece
        part_b[j] = piece.astype(BF16)
    waits = []
    for d in range(1, 4):
        to = (t + d) % 4
        waits.append(links.start(part_b.at[to], part_in.at[d - 1], me.tp(to)))
    arrived(*waits)
    h1 = part_f[t] + resid_ref[:, pl.ds(pl.multiple_of(t * 256, 256), 256)].astype(F32)
    for d in range(3):
        h1 += part_in[d].astype(F32)
    h1 = h1.astype(BF16)
    h_ref[z, y] = h1

    low, high = pl.ds(0, 48), pl.ds(48, 48)

    gain = gain_ref[...].astype(F32).reshape(1, WIDTH)
    lane = lax.broadcasted_iota(jnp.int32, (SPAN, 128), 1)
    squares = [jnp.zeros((SPAN, 128), F32)]

    def rows_of(side, row):
        return jnp.concatenate(
            [h_ref[side * 4 + k, row] for k in range(4)], axis=1
        ).astype(F32)

    def prepare(row):
        for side in range(2):
            rows = rows_of(side, row)
            squares[0] = jnp.where(
                lane == row * 2 + side, jnp.sum(rows * rows, axis=1, keepdims=True), squares[0]
            )
            xs[side, row] = (rows * gain).astype(BF16)

    def along_z(row, seen):
        mine = h_ref.at[z, row]
        right2, left2 = pass_on(mine, me.at_z(2)), pass_on(mine, me.at_z(-2))
        right1, left1 = pass_on(mine, me.at_z(1)), pass_on(mine, me.at_z(-1))
        seen(z)
        yield
        at = (z + 6) % 8
        arrived(right2)
        right3 = pass_on(h_ref.at[at, row], me.at_z(1))
        right4 = pass_on(h_ref.at[at, row, low], me.at_z(2))
        far = (z + 2) % 8
        arrived(left2)
        left3 = pass_on(h_ref.at[far, row], me.at_z(-1))
        left4 = pass_on(h_ref.at[far, row, high], me.at_z(-2))
        arrived(right1)
        seen((z + 7) % 8)
        arrived(left1)
        seen((z + 1) % 8)
        seen(at)
        seen(far)
        yield
        arrived(right4, left4)
        seen((z + 4) % 8)
        arrived(right3)
        seen((z + 5) % 8)
        arrived(left3)
        seen((z + 3) % 8)

    def own_rows():
        waits = {1: [], 3: []}

        def seen(at):
            for d in (1, 3):
                waits[d].append(pass_on(h_ref.at[at, y], me.at_y_step(d)))

        yield from along_z(y, seen)
        prepare(y)
        yield
        arrived(*waits[1])
        prepare((y + 3) % 4)
        arrived(*waits[3])
        prepare((y + 1) % 4)

    def opposite_rows():
        copy = pass_on(h_ref.at[z, y], me.at_y_step(2))
        yield
        arrived(copy)
        yield from along_z((y + 2) % 4, lambda at: None)
        prepare((y + 2) % 4)

    in_turn(opposite_rows(), own_rows())

    chunks = (pl.ds(0, 1024), pl.ds(1024, MAIN))

    def project(side, dst, k):
        rows = xs[side].reshape(4 * SPAN, WIDTH)
        parts = ((gw, 0, MAIN), (rw, MAIN, 128)) if k == 0 else ((uw, 1024, MAIN),)
        for w, base, size in parts:
            out = lax.dot_general(rows, w[0:size], NT, preferred_element_type=F32)
            dst[:, :, :, base : base + size] = out.astype(dst.dtype).reshape(4, 2, 48, size)

    def to_core(k):
        project(1 - c, send_core, k)
        at = (slice(None), slice(None), slice(None), chunks[k])
        return links.start(send_core.at[at], recv_core.at[at], me.core())

    def joined(i, half, cols):
        return keep[i, half, :, cols] + recv_core[i, half, :, cols].astype(F32)

    def push(k, half, slot, i, device):
        cols = chunks[k]
        stage[i, half, :, cols] = joined(i, half, cols).astype(BF16)
        return links.start(
            stage.at[i, half, :, cols], recv_one.at[half, slot, :, cols], device
        )

    def first_step(k):
        return (
            push(k, 0, 1, 3 - me.xa, me.at_x(me.xa)),
            push(k, 1, 1, flip(me.xb), me.at_x(me.xb)),
            push(k, 0, 0, me.xa, me.at_x(me.xa)),
            push(k, 1, 0, me.xb, me.at_x(me.xb)),
        )

    def second_step(k, far, half, i, device):
        cols = chunks[k]
        arrived(far)
        stage[i, half, :, cols] = plus(
            joined(i, half, cols), recv_one[half, 1, :, cols]
        ).astype(BF16)
        return links.start(stage.at[i, half, :, cols], recv_two.at[half, :, cols], device)

    core_0 = to_core(0)
    project(c, keep, 0)
    core_1 = to_core(1)
    arrived(core_0)
    step_0 = first_step(0)
    project(c, keep, 1)
    arrived(core_1)
    step_1 = first_step(1)
    turned = jnp.transpose(jnp.concatenate([squares[0], jnp.zeros((32, 128), F32)], axis=0))
    for g in range(8):
        sq_out[g] = jnp.broadcast_to(turned[g : g + 1], (8, 128))
    sq_waits = []
    for d in range(1, 8):
        to = (f + d) % 8
        sq_waits.append(links.start(sq_out.at[to], sq_in.at[d - 1], me.ffn(to)))
    own_h[...] = rows_of(me.zh, y)
    two_a, two_b = [], []
    for k, step in ((0, step_0), (1, step_1)):
        two_a.append(second_step(k, step[0], 0, me.xb, me.at_x(me.xb)))
        two_b.append(second_step(k, step[1], 1, me.xa, me.at_x(me.xa)))

    arrived(*sq_waits)
    total = sq_out[f]
    for d in range(7):
        total += sq_in[d]
    total = jnp.transpose(jnp.concatenate([total] * 16, axis=0))
    rs = lax.rsqrt(total / D + 1e-06)[:SPAN, 0:1]

    def silu(v):
        return v / (1.0 + jnp.exp(-v))

    def activate(half):
        both = plus(joined(x, half, slice(None)), recv_one[half, 0], recv_two[half])
        both = both * rs[half * 48 : (half + 1) * 48]
        rest = both[:, MAIN:1024]
        hid[c, x, half, :, 0:MAIN] = (silu(both[:, :MAIN]) * both[:, 1024:]).astype(BF16)
        hid[c, x, half, :, MAIN:] = (silu(rest) * pltpu.roll(rest, 64, 1)).astype(BF16)

    def share(half, i, device):
        return pass_on(hid.at[c, i, half], device)

    arrived(step_0[2], step_1[2], *two_a)
    activate(0)
    a0 = share(0, x, me.at_x(me.xa))
    b0 = share(0, x, me.at_x(me.xb))
    core_waits = [share(0, x, me.core())]
    arrived(step_0[3], step_1[3], *two_b)
    activate(1)
    b1 = share(1, x, me.at_x(me.xb))
    a1 = share(1, x, me.at_x(me.xa))
    core_waits.append(share(1, x, me.core()))
    arrived(a0)
    far_0 = share(0, me.xa, me.at_x(me.xb))
    core_waits.append(share(0, me.xa, me.core()))
    arrived(b1)
    far_1 = share(1, me.xb, me.at_x(me.xa))
    core_waits.append(share(1, me.xb, me.core()))
    arrived(b0)
    core_waits.append(share(0, me.xb, me.core()))
    arrived(a1)
    core_waits.append(share(1, me.xa, me.core()))
    load_d.wait()
    arrived(far_0)
    core_waits.append(share(0, flip(me.xb), me.core()))
    arrived(far_1)
    core_waits.append(share(1, flip(me.xb), me.core()))

    def lower(side):
        rows = hid[side].reshape(4 * SPAN, WIDTH)[:, :HID]
        out = jnp.dot(rows, dw[...], preferred_element_type=F32)
        for i in range(4):
            for k in range(4):
                base = i * SPAN + k * ROWS_OUT
                piece = out[base : base + ROWS_OUT].astype(BF16)
                for j in range(2):
                    pieces[side * 4 + k, i, j] = piece[:, j * 512 : (j + 1) * 512]

    lower(c)
    arrived(*core_waits)
    lower(1 - c)

    def along_z_sum(src, near, relay, half, far):
        copies = []
        for way, sign in ((0, 1), (1, -1)):
            copies.append(
                (
                    links.start(src(3 * sign), relay.at[way], me.at_z(sign)),
                    links.start(src(4).at[way], half.at[way], me.at_z(2 * sign)),
                )
            )
        close = [
            links.start(src(sign), near.at[way], me.at_z(sign))
            for way, sign in ((0, 1), (1, -1))
        ]
        yield
        ends = []
        for way, sign in ((0, 1), (1, -1)):
            ref = src(2 * sign)
            arrived(*copies[way])
            ref[1 - way] = plus(ref[1 - way], relay[way, 1 - way]).astype(BF16)
            ref[way] = plus(ref[way], relay[way, way], half[way]).astype(BF16)
            ends.append(links.start(ref, far.at[way], me.at_z(2 * sign)))
        yield
        src(0)
        arrived(*close, *ends)

    def own_sum():
        waits = {}
        for s in (3, 5, 4, 1, 7, 2, 6, 0):
            at = (z + s) % 8
            waits[s] = [
                links.start(
                    pieces.at[at, (y + d) % 4], from_y.at[d // 2, at], me.at_y_step(d)
                )
                for d in (1, 3)
            ]
        yield

        def src(step):
            at = (z + step + 8) % 8
            if step % 8 in waits:
                arrived(*waits.pop(step % 8))
                summed[at] = plus(pieces[at, y], from_y[0, at], from_y[1, at]).astype(BF16)
            return summed.at[at]

        yield from along_z_sum(src, near.at[0], relay.at[0], halves.at[0], far.at[0])

    def opposite_sum():
        row = (y + 2) % 4
        yield from along_z_sum(
            lambda step: pieces.at[(z + step + 8) % 8, row],
            near.at[1], relay.at[1], halves.at[1], far.at[1],
        )
        done[...] = plus(
            pieces[z, row], near[1, 0], near[1, 1], far[1, 0], far[1, 1]
        ).astype(BF16)
        copy = links.start(done, last, me.at_y_step(2))
        yield
        arrived(copy)

    in_turn(opposite_sum(), own_sum())
    total = plus(summed[z], near[0, 0], near[0, 1], far[0, 0], far[0, 1], last[...])
    down = jnp.concatenate([total[0], total[1]], axis=1)
    start = pl.multiple_of(t * ROWS_OUT, 8)
    out = own_h[pl.ds(start, ROWS_OUT), :] + down
    live = start + lax.broadcasted_iota(jnp.int32, (ROWS_OUT, WIDTH), 0) < length
    out_ref[...] = jnp.where(live, out, 0.0).astype(BF16)
    links.finish()


def layer_call(*args):
    vmem = pl.BlockSpec(memory_space=pltpu.VMEM)
    smem = pl.BlockSpec(memory_space=pltpu.SMEM)
    hbm = pl.BlockSpec(memory_space=pl.ANY)
    copies = 14 + 7 + 3 + 33 + 2 + 7 + 12 + 14 + 33
    piece = (2, ROWS_OUT, 512)
    block = (4, 2, 48, BOTH)
    return pl.pallas_call(
        layer_kernel,
        out_shape=jax.ShapeDtypeStruct((ROWS_OUT, WIDTH), BF16),
        in_specs=[smem, smem, vmem] + [hbm] * 8,
        out_specs=vmem,
        scratch_shapes=[
            pltpu.VMEM((SPAN, 2048), BF16),
            pltpu.VMEM((2, SPAN, 256), BF16),
            pltpu.VMEM((SPAN, WIDTH), BF16),
            pltpu.VMEM((2, KEYS, 256), BF16),
            pltpu.VMEM((2048, WIDTH), BF16),
            pltpu.VMEM((HID, WIDTH), BF16),
            pltpu.VMEM((HID, WIDTH), BF16),
            pltpu.VMEM((128, WIDTH), BF16),
            pltpu.VMEM((HID, WIDTH), BF16),
            pltpu.VMEM((8, 2, SPAN, DH), BF16),
            pltpu.VMEM((8, 2, 8, 128), F32),
            pltpu.VMEM((8, 2, SPAN, DH), BF16),
            pltpu.VMEM((8, 2, 8, 128), F32),
            pltpu.VMEM((8, 2, SPAN, DH), BF16),
            pltpu.VMEM((4, SPAN, 256), F32),
            pltpu.VMEM((4, SPAN, 256), BF16),
            pltpu.VMEM((3, SPAN, 256), BF16),
            pltpu.VMEM((8, 4, SPAN, 256), BF16),
            pltpu.VMEM((2, 4, SPAN, WIDTH), BF16),
            pltpu.VMEM((SPAN, WIDTH), F32),
            pltpu.VMEM((8, 8, 128), F32),
            pltpu.VMEM((7, 8, 128), F32),
            pltpu.VMEM(block, BF16),
            pltpu.VMEM(block, BF16),
            pltpu.VMEM(block, F32),
            pltpu.VMEM(block, BF16),
            pltpu.VMEM((2, 2, 48, BOTH), BF16),
            pltpu.VMEM((2, 48, BOTH), BF16),
            pltpu.VMEM((2, 4, 2, 48, WIDTH), BF16),
            pltpu.VMEM((8, 4) + piece, BF16),
            pltpu.VMEM((2, 8) + piece, BF16),
            pltpu.VMEM((8,) + piece, BF16),
            pltpu.VMEM((2, 2) + piece, BF16),
            pltpu.VMEM((2, 2) + piece, BF16),
            pltpu.VMEM((2, 2, ROWS_OUT, 512), BF16),
            pltpu.VMEM((2, 2) + piece, BF16),
            pltpu.VMEM(piece, BF16),
            pltpu.VMEM(piece, BF16),
            pltpu.SemaphoreType.DMA((9,)),
            pltpu.SemaphoreType.DMA((copies,)),
            pltpu.SemaphoreType.DMA((copies,)),
        ],
        compiler_params=pltpu.CompilerParams(
            collective_id=0, has_side_effects=True, vmem_limit_bytes=60 << 20
        ),
        name="layer",
    )(*args)


def body(
    queries,
    new_kv,
    kv_cache,
    lengths,
    prefixes,
    resid,
    out_weight,
    gain,
    gate_weight,
    up_weight,
    down_weight,
):
    return layer_call(
        lengths,
        prefixes,
        gain,
        queries,
        new_kv,
        resid,
        kv_cache,
        out_weight,
        gate_weight.T,
        up_weight.T,
        down_weight,
    )


def solution(mesh):
    return jax.shard_map(
        body,
        mesh=mesh,
        in_specs=(
            P("grp", "tp"),
            P(None, "grp", "tp"),
            P(None, "grp", "ffn", "tp"),
            P("grp"),
            P("grp"),
            P("grp", "ffn"),
            P("tp", "ffn"),
            P("ffn"),
            P("ffn", ("grp", "tp")),
            P("ffn", ("grp", "tp")),
            P(("grp", "tp"), "ffn"),
        ),
        out_specs=P(("grp", "tp"), "ffn"),
        check_vma=False,
    )
```
